32 devices in a mesh: rep: 2 (over y), lat: 16 (over z, x, core).
Axes of the slice: x: 2, y: 2, z: 4, core: 2. Of those that a mesh axis runs over, the one named last changes fastest.
Arguments:
- block_input: bfloat16 [32, 180, 768], P(('rep', 'lat')), parts along dimension 0, may hold values from -6 to 6
- cotangent: bfloat16 [32, 180, 768], P(('rep', 'lat')), parts along dimension 0, may hold values from -8 to 8
- first_gain: float32 [768], replicated, may hold values from 0.5 to 1.5
- first_shift: float32 [768], replicated, may hold values from -1.25 to 1.25
- inner_weight: float32 [2, 768, 96], replicated, may hold values from -0.4375 to 0.4375
- inner_bias: float32 [2, 768], replicated, may hold values from -3 to 3
- outer_weight: float32 [2, 768, 96], replicated, may hold values from -0.4375 to 0.4375
- outer_bias: float32 [2, 768], replicated, may hold values from -0.125 to 0.125
- second_gain: float32 [768], replicated, may hold values from 0.5 to 1.5
- second_shift: float32 [768], replicated, may hold values from -1.25 to 1.25
- up_weight: bfloat16 [3072, 768], replicated, may hold values from -0.21875 to 0.21875
- up_bias: float32 [3072], replicated, may hold values from -3 to 3
- down_weight: bfloat16 [768, 3072], replicated, may hold values from -0.109375 to 0.109375
- down_bias: float32 [768], replicated, may hold values from -1.75 to 1.75
Outputs:
- block_output: bfloat16 [32, 180, 768], P(('rep', 'lat')), parts along dimension 0
- input_grad: bfloat16 [32, 180, 768], P(('rep', 'lat')), parts along dimension 0
- up_grad: float32 [6144, 768], P(('rep', 'lat')), parts along dimension 0
- down_grad: float32 [1536, 3072], P(('rep', 'lat')), parts along dimension 0
- inner_grad: float32 [4, 768, 96], P('rep', 'lat'), parts along dimension 0
- outer_grad: float32 [4, 768, 96], P('rep', 'lat'), parts along dimension 0
The draws below stay inside these ranges and needn't reach their ends.
There are 2 independent parts, one for each index of `rep`. The reference program is written for one: setup_inputs(seed, part) draws one part's arguments, and reference() takes and returns one part's arrays. A program takes and returns all parts, laid end to end along the dimension named above; an argument that names none is the same for every part. Nothing has to cross between parts.
All inputs are finite; a program needn't handle non-finite values.
Results may differ from the reference program's by a relative error of at most 0.017.
Values may be sent and summed in bfloat16 or wider, within the bound.
No kernel may reach another device: no remote copies, remote signals or barrier semaphores. Data moves between devices by JAX's collectives and lax.ppermute only.
A program may use at most 128 MiB of HBM per device.

```python
from functools import partial
import jax
import jax.numpy as jnp
from jax import lax

D = 768
FF = 3072
W = 180
BS = 96
H = 16


def strengthened(array, stream_key, source, target, parts, factor):
    def block_of(position):
        return (jnp.arange(array.shape[position]) // (array.shape[position] // parts)).reshape((-1,) + (1,) * (array.ndim - 1 - position))

    one_side = jax.random.permutation(stream_key, parts)[block_of(target)]
    second = (block_of(target) + parts // 2) % parts
    return jnp.where((block_of(source) == one_side) | (block_of(source) == second), factor * array, array)


def level_of(rng, shape, split, smallest, top_value):
    gain, own = 1.0, jax.random.fold_in(rng, 6)
    for axis_at, blocks in split:
        heights = jnp.exp(jax.random.uniform(jax.random.fold_in(own, axis_at), (blocks,), jnp.float32, smallest / len(split), top_value / len(split)))
        gain = gain * jnp.repeat(heights, shape[axis_at] // blocks).reshape([-1 if axis == axis_at else 1 for axis in range(len(shape))])
    return gain


def gaussian(key, shape, width, bound, cuts=(), kind=jnp.bfloat16):
    loudness = level_of(key, shape, cuts, -0.22, 0.18) if cuts else 1.0
    values = jax.random.normal(key, shape, jnp.float32) * width * loudness
    return jnp.minimum(jnp.maximum(values, -bound), bound).astype(kind)


def gaussian_with(key, dims, deviation, limit, cuts, heavy, kind=jnp.bfloat16):
    drawn = deviation * jax.random.normal(key, dims, jnp.float32)
    if cuts:
        drawn = drawn * level_of(key, dims, cuts, -0.22, 0.18)
    return jnp.clip(strengthened(drawn, jax.random.fold_in(key, 3), *heavy), -limit, limit).astype(kind)


def setup_inputs(seed: int = 0, part: int = 0) -> dict:
    key_of = jax.random.split(jax.random.key(seed), 15)
    part_keys = jax.random.split(jax.random.fold_in(key_of[14], part), 15)
    return {
        "block_input": gaussian(part_keys[0], (H, W, D), 1.0, 6.0, ((0, 16),)),
        "cotangent": gaussian_with(part_keys[1], (H, W, D), 1.0, 8.0, ((0, 16),), (0, 2, 16, 2.0)),
        "first_gain": jnp.clip(1.0 + 0.1 * jax.random.normal(key_of[2], (D,), jnp.float32), 0.5, 1.5),
        "first_shift": gaussian(key_of[3], (D,), 0.2, 1.25, (), jnp.float32),
        "inner_weight": gaussian(key_of[4], (2, D, BS), (2 * BS) ** -0.5, 0.4375, (), jnp.float32),
        "inner_bias": gaussian(key_of[5], (2, D), 0.5, 3.0, (), jnp.float32),
        "outer_weight": gaussian(key_of[6], (2, D, BS), (2 * BS) ** -0.5, 0.4375, (), jnp.float32),
        "outer_bias": gaussian(key_of[7], (2, D), 0.02, 0.125, (), jnp.float32),
        "second_gain": jnp.clip(1.0 + 0.1 * jax.random.normal(key_of[8], (D,), jnp.float32), 0.5, 1.5),
        "second_shift": gaussian(key_of[9], (D,), 0.2, 1.25, (), jnp.float32),
        "up_weight": gaussian(key_of[10], (FF, D), D ** -0.5, 0.21875),
        "up_bias": gaussian(key_of[11], (FF,), 0.5, 3.0, (), jnp.float32),
        "down_weight": gaussian(key_of[12], (D, FF), FF ** -0.5, 0.109375),
        "down_bias": gaussian(key_of[13], (D,), 0.3, 1.75, (), jnp.float32),
    }


EPS = 1e-05
SHRINK = 0.01

def layer_norm(values, scaling, offset):
    average = lax.optimization_barrier(jnp.mean(values, axis=-1, keepdims=True))
    centered = values - average
    variance = lax.optimization_barrier(jnp.mean(centered * centered, axis=-1, keepdims=True))
    return centered * lax.rsqrt(variance + EPS) * scaling + offset

def gelu_exact(values):
    return jax.nn.gelu(values, approximate=False)

def block_mix(real_part, imag_part, weight, offset):
    leading = real_part.shape[:-1]
    features = weight.shape[1]
    block_size = weight.shape[2]
    blocks = features // block_size
    weight_re = weight[0].reshape(blocks, block_size, block_size)
    weight_im = weight[1].reshape(blocks, block_size, block_size)
    real_blocks = real_part.reshape(leading + (blocks, block_size))
    imag_blocks = imag_part.reshape(leading + (blocks, block_size))
    mixing = partial(jnp.einsum, '...bi,bio->...bo', precision=lax.Precision.HIGHEST)
    out_real = mixing(real_blocks, weight_re) - mixing(imag_blocks, weight_im)
    out_imag = mixing(imag_blocks, weight_re) + mixing(real_blocks, weight_im)
    return (out_real.reshape(leading + (features,)) + offset[0], out_imag.reshape(leading + (features,)) + offset[1])

def soft_threshold(values):
    return values - SHRINK * jnp.tanh(values / SHRINK)

def spectral_mlp(real_part, imag_part, inner_weight, inner_bias, outer_weight, outer_bias):
    hidden_re, hidden_im = block_mix(real_part, imag_part, inner_weight, inner_bias)
    hidden_re = gelu_exact(hidden_re)
    hidden_im = gelu_exact(hidden_im)
    out_re, out_im = block_mix(hidden_re, hidden_im, outer_weight, outer_bias)
    return (soft_threshold(out_re), soft_threshold(out_im))

def rounded(values):
    return lax.optimization_barrier(values.astype(jnp.bfloat16)).astype(jnp.float32)

def spectral_filter(normed, inner_weight, inner_bias, outer_weight, outer_bias):
    along_lon = jnp.fft.rfft(normed, axis=1, norm='ortho')
    lon_re = rounded(jnp.real(along_lon))
    lon_im = rounded(jnp.imag(along_lon))
    spectrum = jnp.fft.fft(lax.complex(lon_re, lon_im), axis=0, norm='ortho')
    mixed_real_part, mixed_im = spectral_mlp(jnp.real(spectrum), jnp.imag(spectrum), inner_weight, inner_bias, outer_weight, outer_bias)
    returned = jnp.fft.ifft(lax.complex(mixed_real_part, mixed_im), axis=0, norm='ortho')
    back_re = rounded(jnp.real(returned))
    back_im = rounded(jnp.imag(returned))
    spatial_domain = jnp.fft.irfft(lax.complex(back_re, back_im), n=W, axis=1, norm='ortho')
    return spatial_domain + normed

def reference(block_input, cotangent, first_gain, first_shift, inner_weight, inner_bias, outer_weight, outer_bias, second_gain, second_shift, up_weight, up_bias, down_weight, down_bias):

    def first_half(values, weight_a, weight_b):
        normed = layer_norm(values, first_gain, first_shift)
        return spectral_filter(normed, weight_a, inner_bias, weight_b, outer_bias)
    grid_shape = block_input.shape
    input_f32 = block_input.astype(jnp.float32)
    filtered, filter_vjp = jax.vjp(first_half, input_f32, inner_weight, outer_weight)
    residual = (input_f32 + filtered).astype(jnp.bfloat16)
    residual_f32 = residual.astype(jnp.float32)
    normed_two, norm_vjp = jax.vjp(lambda values: layer_norm(values, second_gain, second_shift), residual_f32)
    flat_normed = normed_two.astype(jnp.bfloat16).reshape(-1, D)
    pre_act = jnp.einsum('td,fd->tf', flat_normed, up_weight, preferred_element_type=jnp.float32) + up_bias
    hidden_f32, gelu_vjp = jax.vjp(gelu_exact, pre_act)
    hidden = hidden_f32.astype(jnp.bfloat16)
    outcome = jnp.einsum('tf,df->td', hidden, down_weight, preferred_element_type=jnp.float32) + down_bias
    block_output = (residual_f32.reshape(-1, D) + outcome).astype(jnp.bfloat16).reshape(grid_shape)
    grad_flat = cotangent.reshape(-1, D)
    down_grad = jnp.einsum('td,tf->df', grad_flat, hidden, preferred_element_type=jnp.float32)
    grad_hidden = jnp.einsum('td,df->tf', grad_flat, down_weight, preferred_element_type=jnp.float32)
    grad_pre = gelu_vjp(grad_hidden)[0].astype(jnp.bfloat16)
    up_grad = jnp.einsum('tf,td->fd', grad_pre, flat_normed, preferred_element_type=jnp.float32)
    grad_second = jnp.einsum('tf,fd->td', grad_pre, up_weight, preferred_element_type=jnp.float32).reshape(grid_shape)
    grad_resid = cotangent.astype(jnp.float32) + norm_vjp(grad_second)[0]
    grad_values, inner_grad, outer_grad = filter_vjp(grad_resid)
    input_grad = (grad_resid + grad_values).astype(jnp.bfloat16)
    return (block_output, input_grad, up_grad, down_grad, inner_grad, outer_grad)
```

```python
from functools import partial
import math

import jax
import jax.numpy as jnp
import ml_dtypes
import numpy as np
from jax import lax
from jax.experimental import pallas as pl
from jax.experimental.pallas import tpu as pltpu
from jax.sharding import PartitionSpec as P

EPS = 1e-05
SHRINK = 0.01
LANES = 128
BF16 = jnp.bfloat16
F32 = jnp.float32


def dot(a, b, dims=((1,), (0,))):
    return lax.dot_general(a, b, (dims, ((), ())), preferred_element_type=F32)


def split(values):
    high = values.astype(BF16)
    return high, (values - high.astype(F32)).astype(BF16)


def dot3(a, b):
    return dot(a[0], b[0]) + (dot(a[0], b[1]) + dot(a[1], b[0]))


def host_split(table):
    high = table.astype(np.float32).astype(ml_dtypes.bfloat16)
    low = (table - high.astype(np.float64)).astype(np.float32).astype(ml_dtypes.bfloat16)
    return jnp.asarray(np.stack((high, low)))


def lon_table(length, members, per_member, weighted):
    count = length // 2 + 1
    mode = np.arange(members * per_member).reshape(members, 1, per_member, 1)
    angle = 2.0 * np.pi / length * ((mode * np.arange(length)) % length)
    weight = (mode < count) / math.sqrt(length)
    edge = (mode == 0) | (2 * mode == length)
    if weighted:
        weight = weight * np.where(edge, 1.0, 2.0)
    sine = np.where(edge, 0.0, -np.sin(angle))
    table = np.concatenate((np.cos(angle) * weight, sine * weight), axis=1)
    return table.reshape(members * 2 * per_member, length)


def moments(values):
    average = jnp.mean(values, axis=-1, keepdims=True)
    centered = values - average
    variance = jnp.mean(centered * centered, axis=-1, keepdims=True)
    scale = lax.rsqrt(variance + EPS)
    return centered * scale, scale


def norm_grad(unit, scale, grad_unit):
    mean_grad = jnp.mean(grad_unit, axis=-1, keepdims=True)
    mean_dot = jnp.mean(grad_unit * unit, axis=-1, keepdims=True)
    return scale * (grad_unit - mean_grad - unit * mean_dot)


def gelu_and_slope(values):
    magnitude = jnp.abs(values) * math.sqrt(0.5)
    t = 1.0 / (1.0 + 0.3275911 * magnitude)
    bell = jnp.exp(-0.5 * values * values)
    tail = t * (0.127414796 + t * (-0.142248368 + t * (0.7107068705 + t * (-0.7265760135 + t * 0.5307027145))))
    tail = tail * bell
    phi = jnp.where(values < 0.0, tail, 1.0 - tail)
    return values * phi, phi + values * (bell * (1.0 / math.sqrt(2.0 * math.pi)))


def fft(pairs, sign):
    n = len(pairs)
    if n == 1:
        return pairs
    assert n % 2 == 0
    even, odd = fft(pairs[0::2], sign), fft(pairs[1::2], sign)
    low, high = [], []
    for k in range(n // 2):
        (er, ei), (xr, xi) = even[k], odd[k]
        if k == 0:
            tr, ti = xr, xi
        elif 4 * k == n:
            tr, ti = (-xi, xr) if sign > 0 else (xi, -xr)
        else:
            c, s = math.cos(2.0 * math.pi * k / n), sign * math.sin(2.0 * math.pi * k / n)
            tr, ti = xr * c - xi * s, xr * s + xi * c
        low.append((er + tr, ei + ti))
        high.append((er - tr, ei - ti))
    return low + high


def spread(values, block):
    zeros = jnp.zeros((values.shape[0], LANES - block), values.dtype)
    pieces = []
    for b in range(values.shape[1] // block):
        pieces += [jnp.concatenate((values[:, b * block:(b + 1) * block], zeros), axis=1)]
    return jnp.concatenate(pieces, axis=1)


def compact(values, block, blocks):
    return jnp.concatenate([values[:, b * LANES:b * LANES + block] for b in range(blocks)], axis=1)


def lane_mask(shape, low, high):
    lane = lax.broadcasted_iota(jnp.int32, shape, 1)
    return (lane >= low) & (lane < high)


def pack(values, block):
    rows = values.shape[0]
    free = LANES - block
    kept = rows * block // LANES
    spare = rows - kept
    out = []
    for k in range(kept // spare):
        moved = pltpu.roll(values[kept:], block - k * free, 1)
        own = values[k * spare:(k + 1) * spare]
        out.append(jnp.where(lane_mask(own.shape, 0, block), own, moved))
    return jnp.concatenate(out, axis=0)


def unpack(values, block):
    kept = values.shape[0]
    free = LANES - block
    spare = kept * free // block
    last = jnp.zeros((spare, LANES), values.dtype)
    for k in range(kept // spare):
        moved = pltpu.roll(values[k * spare:(k + 1) * spare], LANES - block + k * free, 1)
        last = jnp.where(lane_mask(moved.shape, k * free, (k + 1) * free), moved, last)
    first = jnp.where(lane_mask(values.shape, 0, block), values, 0.0)
    return jnp.concatenate((first, last), axis=0)


def gather_blocks(ref, members, block, out_ref):
    devices = ref.shape[0]
    rows = out_ref.shape[0] // members
    for d in range(devices):
        b, r = d // members, d % members
        out_ref[r * rows:(r + 1) * rows, b * LANES:(b + 1) * LANES] = unpack(ref[d].astype(F32), block).astype(BF16)
    return out_ref[...]


def scatter_blocks(values, members, block, ref):
    rows = values.shape[0] // members
    for d in range(ref.shape[0]):
        b, r = d // members, d % members
        piece = values[r * rows:(r + 1) * rows, b * LANES:(b + 1) * LANES]
        ref[d] = pack(piece, block).astype(BF16)


def pad_rows(values, rows):
    return jnp.concatenate((values, jnp.zeros((rows - values.shape[0], values.shape[1]), values.dtype)), axis=0)


def fetch(pairs, sems):
    copies = [pltpu.make_async_copy(src, dst, sems.at[i]) for i, (src, dst) in enumerate(pairs)]
    for copy in copies:
        copy.start()
    return copies


def first_kernel(members, block, x_hbm, gain_ref, shift_ref, table_hbm, out_ref, x_ref, table_ref, sems):
    x_copy, table_copy = fetch(((x_hbm, x_ref), (table_hbm, table_ref)), sems)
    x_copy.wait()
    unit, _ = moments(x_ref[...].astype(F32))
    first = unit * gain_ref[...][None] + shift_ref[...][None]
    wide = split(spread(pad_rows(first, table_ref.shape[2]), block))
    table_copy.wait()
    scatter_blocks(dot3((table_ref[0], table_ref[1]), wide), members, block, out_ref)


def load_transform(ref, block, sign, wide_ref, rows_ref):
    devices, rows, _ = rows_ref.shape
    half = rows // 2
    factor = 1.0 / math.sqrt(devices)
    for h in range(devices):
        rows_ref[h] = unpack(ref[h].astype(F32) * factor, block)
    for row in range(0, half, 8):
        pairs = [(rows_ref[h, row:row + 8], rows_ref[h, half + row:half + row + 8]) for h in range(devices)]
        for h, (re, im) in enumerate(fft(pairs, sign)):
            wide_ref[h * half + row:h * half + row + 8, :LANES] = re
            wide_ref[h * half + row:h * half + row + 8, LANES:] = im


def store_transform(wide_ref, block, sign, ref, rows_ref):
    devices, rows, _ = rows_ref.shape
    half = rows // 2
    factor = 1.0 / math.sqrt(devices)
    for row in range(0, half, 8):
        pairs = [
            (wide_ref[h * half + row:h * half + row + 8, :LANES], wide_ref[h * half + row:h * half + row + 8, LANES:])
            for h in range(devices)
        ]
        for h, (re, im) in enumerate(fft(pairs, sign)):
            rows_ref[h, row:row + 8] = re
            rows_ref[h, half + row:half + row + 8] = im
    for h in range(devices):
        ref[h] = (pack(rows_ref[h], block) * factor).astype(BF16)


def filter_kernel(block, in_ref, w1h_ref, w1l_ref, b1_ref, w2h_ref, w2l_ref, b2_ref,
                  out_ref, spec_ref, hid_ref, slope_ref, shrink_ref, wide_ref, rows_ref):
    load_transform(in_ref, block, -1.0, wide_ref, rows_ref)
    spectrum = split(wide_ref[...])
    spec_ref[...] = spectrum[0]
    pre = dot3(spectrum, (w1h_ref[...], w1l_ref[...])) + b1_ref[...]
    inner, slope = gelu_and_slope(pre)
    slope_ref[...] = slope.astype(BF16)
    inner = split(inner)
    hid_ref[...] = inner[0]
    outer = dot3(inner, (w2h_ref[...], w2l_ref[...])) + b2_ref[...]
    bend = jnp.tanh(outer / SHRINK)
    shrink_ref[...] = (bend * bend).astype(BF16)
    wide_ref[...] = outer - SHRINK * bend
    store_transform(wide_ref, block, 1.0, out_ref, rows_ref)


def complex_grad(grad, block):
    a, b = slice(0, block), slice(LANES, LANES + block)
    return grad[a, a] + grad[b, b], grad[a, b] - grad[b, a]


def filter_grad_kernel(block, in_ref, w1_ref, w2_ref, spec_ref, hid_ref, slope_ref, shrink_ref,
                       out_ref, grads_ref, wide_ref, rows_ref):
    load_transform(in_ref, block, -1.0, wide_ref, rows_ref)
    grad_outer = (wide_ref[...] * shrink_ref[...].astype(F32)).astype(BF16)
    grad_inner = dot(grad_outer, w2_ref[...], ((1,), (1,)))
    grad_pre = (grad_inner * slope_ref[...].astype(F32)).astype(BF16)
    wide_ref[...] = dot(grad_pre, w1_ref[...], ((1,), (1,)))
    store_transform(wide_ref, block, 1.0, out_ref, rows_ref)
    re, im = complex_grad(dot(spec_ref[...], grad_pre, ((0,), (0,))), block)
    grads_ref[0, 0] = re
    grads_ref[0, 1] = im
    re, im = complex_grad(dot(hid_ref[...], grad_outer, ((0,), (0,))), block)
    grads_ref[1, 0] = re
    grads_ref[1, 1] = im


def second_kernel(members, block, blocks, in_ref, x_ref, gain1_ref, shift1_ref, gain2_ref, shift2_ref, table_hbm,
                  resid_ref, second_ref, rows_ref, table_ref, sems):
    (table_copy,) = fetch(((table_hbm, table_ref),), sems)
    back = gather_blocks(in_ref, members, block, rows_ref)
    x = x_ref[...].astype(F32)
    unit, _ = moments(x)
    x = pad_rows(x + (unit * gain1_ref[...][None] + shift1_ref[...][None]), resid_ref.shape[0])
    table_copy.wait()
    filtered = compact(dot(table_ref[0], back) + dot(table_ref[1], back), block, blocks)
    residual = (x + filtered).astype(BF16)
    resid_ref[...] = residual
    unit, _ = moments(residual.astype(F32))
    second = unit * gain2_ref[...][None] + shift2_ref[...][None]
    second_ref[...] = pad_rows(second[:x_ref.shape[0]], resid_ref.shape[0]).astype(BF16)


def mlp_kernel(members, block, chunk, second_ref, cot_ref, resid_ref, gain_ref, up_ref, upb_ref, ghid_ref, table_hbm,
               hid_ref, gres_ref, out_ref, acc_ref, table_ref, sems):
    (table_copy,) = fetch(((table_hbm, table_ref),), sems)
    for start in range(0, up_ref.shape[0], chunk):
        part = slice(start, start + chunk)
        pre = dot(second_ref[...], up_ref[part], ((1,), (1,))) + upb_ref[:, part]
        hidden, slope = gelu_and_slope(pre)
        hid_ref[:, part] = hidden.astype(BF16)
        grad_pre = (ghid_ref[:, part] * slope).astype(BF16)
        term = dot(grad_pre, up_ref[part])
        if start == 0:
            acc_ref[...] = term
        else:
            acc_ref[...] += term
    unit, scale = moments(resid_ref[...].astype(F32))
    grad = cot_ref[...].astype(F32) + norm_grad(unit, scale, acc_ref[...] * gain_ref[...][None])
    gres_ref[...] = grad
    wide = split(spread(grad, block))
    table_copy.wait()
    scatter_blocks(dot3((table_ref[0], table_ref[1]), wide), members, block, out_ref)


def last_kernel(members, block, blocks, in_ref, x_ref, gain_ref, gres_ref, table_hbm, out_ref, rows_ref, table_ref,
                sems):
    (table_copy,) = fetch(((table_hbm, table_ref),), sems)
    back = gather_blocks(in_ref, members, block, rows_ref)
    unit, scale = moments(x_ref[...].astype(F32))
    length = unit.shape[0]
    gres = gres_ref[:length]
    table_copy.wait()
    grad = compact(dot(table_ref[0], back) + dot(table_ref[1], back), block, blocks)[:length]
    out_ref[...] = (gres + norm_grad(unit, scale, (grad + gres) * gain_ref[...][None])).astype(BF16)


def down_part_kernel(second_ref, cot_ref, up_ref, bias_ref, out_ref, acc_ref):
    step = pl.program_id(0)
    tokens = second_ref.shape[0] * second_ref.shape[1]
    second = second_ref[...].reshape(tokens, -1)
    hidden, _ = gelu_and_slope(dot(second, up_ref[...], ((1,), (1,))) + bias_ref[...])
    term = dot(hidden.astype(BF16), cot_ref[...].reshape(tokens, -1), ((0,), (0,)))

    @pl.when(step == 0)
    def _():
        acc_ref[...] = term

    @pl.when(step > 0)
    def _():
        acc_ref[...] += term

    @pl.when(step == pl.num_programs(0) - 1)
    def _():
        out_ref[...] = acc_ref[...].T.astype(BF16)


def up_part_kernel(second_ref, cot_ref, up_ref, bias_ref, down_ref, out_ref):
    step = pl.program_id(0)
    tokens = second_ref.shape[0] * second_ref.shape[1]
    second = second_ref[...].reshape(tokens, -1)
    _, slope = gelu_and_slope(dot(second, up_ref[...], ((1,), (1,))) + bias_ref[...])
    grad_pre = (dot(cot_ref[...].reshape(tokens, -1), down_ref[...]) * slope).astype(BF16)
    term = dot(grad_pre, second, ((0,), (0,)))

    @pl.when(step == 0)
    def _():
        out_ref[...] = term

    @pl.when(step > 0)
    def _():
        out_ref[...] += term


def struct(shape, dtype):
    return jax.ShapeDtypeStruct(shape, dtype)


VMEM = pl.BlockSpec(memory_space=pltpu.VMEM)
HBM = pl.BlockSpec(memory_space=pl.ANY)


def call(kernel, out, scratch, in_specs, *args, limit=24):
    return pl.pallas_call(
        kernel, out_shape=out, scratch_shapes=scratch, in_specs=in_specs,
        compiler_params=pltpu.CompilerParams(vmem_limit_bytes=limit << 20))(*args)


def ring_order(devices):
    width = devices // 8
    chips = []
    for row in range(4):
        columns = list(range(1, width))
        chips += [row * width + c for c in (columns if row % 2 == 0 else columns[::-1])]
    chips += [row * width for row in (3, 2, 1, 0)]
    return [2 * chip + core for chip in chips for core in (0, 1)]


def complex_weight(weight, block):
    pad = ((0, LANES - block), (0, LANES - block))
    re, im = jnp.pad(weight[0], pad), jnp.pad(weight[1], pad)
    return jnp.concatenate((jnp.concatenate((re, im), 1), jnp.concatenate((-im, re), 1)), 0)


def shards(
    block_input,
    cotangent,
    first_gain,
    first_shift,
    inner_weight,
    inner_bias,
    outer_weight,
    outer_bias,
    second_gain,
    second_shift,
    up_weight,
    up_bias,
    down_weight,
    down_bias,
):
    bands, length, channels = block_input.shape
    assert bands == 1
    devices = lax.axis_size("lat")
    index = lax.axis_index("lat")
    block = inner_weight.shape[2]
    blocks = channels // block
    members = devices // blocks
    per_member = -(-(length // 2 + 1) // members)
    per_member = -(-per_member // 16) * 16
    rows = 2 * per_member
    units = up_weight.shape[0]
    tokens = -(-length // 64) * 64
    x = block_input[0]
    cot = jnp.pad(cotangent[0], ((0, tokens - length), (0, 0)))
    ring = [ring_order(devices)]
    all_gather = partial(lax.all_gather, axis_name="lat", axis=0, axis_index_groups=ring)
    a2a = partial(lax.all_to_all, axis_name="lat", split_axis=0, concat_axis=0, tiled=True)
    cot_all = all_gather(cot)

    fwd = np.pad(lon_table(length, members, per_member, False), ((0, 0), (0, tokens - length)))
    inv = np.pad(lon_table(length, members, per_member, True), ((0, 0), (0, tokens - length)))
    all_rows, wide = members * rows, blocks * LANES
    packed = struct((devices, rows * block // LANES, LANES), BF16)
    row_scratch = pltpu.VMEM((all_rows, wide), BF16)
    table_scratch = pltpu.VMEM((2, all_rows, tokens), BF16)
    back_scratch = pltpu.VMEM((2, tokens, all_rows), BF16)
    sems = pltpu.SemaphoreType.DMA((2,))

    start = (index // members) * block
    def own(array):
        return lax.dynamic_slice_in_dim(array, start, block, 1)
    w1 = split(complex_weight(own(inner_weight), block))
    w2 = split(complex_weight(own(outer_weight), block))
    b1 = jnp.pad(own(inner_bias), ((0, 0), (0, LANES - block))).reshape(1, 2 * LANES)
    b2 = jnp.pad(own(outer_bias), ((0, 0), (0, LANES - block))).reshape(1, 2 * LANES)
    grad_hidden = dot(cot, down_weight)

    outgoing = call(
        partial(first_kernel, members, block), packed,
        [pltpu.VMEM((length, channels), BF16), table_scratch, sems], [HBM, VMEM, VMEM, HBM],
        x, first_gain, first_shift, host_split(fwd))
    incoming = a2a(outgoing)
    spectral = struct((devices * per_member, 2 * LANES), BF16)
    spectral_scratch = [
        pltpu.VMEM((devices * per_member, 2 * LANES), F32), pltpu.VMEM((devices, rows, LANES), F32)]
    returning, spec, hid, slope, bend = call(
        partial(filter_kernel, block), (packed, spectral, spectral, spectral, spectral), spectral_scratch,
        [VMEM] * 7, incoming, *w1, b1, *w2, b2)
    back = a2a(returning)
    token = struct((tokens, channels), BF16)
    residual, second = call(
        partial(second_kernel, members, block, blocks), (token, token), [row_scratch, back_scratch, sems],
        [VMEM] * 6 + [HBM],
        back, x, first_gain, first_shift, second_gain, second_shift, host_split(inv.T))

    chunk = 512
    hidden, grad_resid, grad_out = call(
        partial(mlp_kernel, members, block, chunk),
        (struct((tokens, units), BF16), struct((tokens, channels), F32), packed),
        [pltpu.VMEM((tokens, channels), F32), table_scratch, sems], [VMEM] * 7 + [HBM],
        second, cot, residual, second_gain, up_weight, up_bias[None], grad_hidden, host_split(inv), limit=32)
    grad_in = a2a(grad_out)
    second_out, cot_all, _ = lax.optimization_barrier((second, cot_all, grad_out))
    second_all = all_gather(second_out)
    block_output = (
        residual.astype(F32) + dot(hidden, down_weight, ((1,), (1,))) + down_bias
    ).astype(BF16)[None, :length]

    grad_back, terms = call(
        partial(filter_grad_kernel, block), (packed, struct((2, 2, block, block), F32)), spectral_scratch,
        [VMEM] * 7, grad_in, w1[0], w2[0], spec, hid, slope, bend)
    grad_lon = a2a(grad_back)
    input_grad = call(
        partial(last_kernel, members, block, blocks), struct((length, channels), BF16),
        [row_scratch, back_scratch, sems], [VMEM] * 4 + [HBM],
        grad_lon, x, first_gain, grad_resid, host_split(fwd.T))[None]

    part = block // members
    terms = terms.reshape(2, 2, members, part, block)
    member = index % members
    def piece(which):
        return lax.dynamic_index_in_dim(terms, which, 2, keepdims=False)
    total = piece(member)
    for hop in range(1, members):
        pairs = [(d, d - d % members + (d % members + hop) % members) for d in range(devices)]
        total = total + lax.ppermute(piece((member + hop) % members), "lat", pairs)

    share = units // devices
    up_own = lax.dynamic_slice_in_dim(up_weight, index * share, share, 0)
    bias_own = lax.dynamic_slice_in_dim(up_bias, index * share, share, 0)[None]
    down_own = lax.dynamic_slice_in_dim(down_weight, index * share, share, 1)
    group = 4 if devices % 4 == 0 else 1
    whole = lambda shape: pl.BlockSpec(shape, lambda i: (0,) * len(shape))
    gathered = pl.BlockSpec((group, tokens, channels), lambda i: (i, 0, 0))
    params = pltpu.CompilerParams(vmem_limit_bytes=24 << 20)
    down_part = pl.pallas_call(
        down_part_kernel, grid=(devices // group,),
        in_specs=[gathered, gathered, whole((share, channels)), whole((1, share))],
        out_specs=whole((channels, share)), out_shape=struct((channels, share), BF16),
        scratch_shapes=[pltpu.VMEM((share, channels), F32)], compiler_params=params,
    )(second_all, cot_all, up_own, bias_own)
    down_rows = a2a(down_part.reshape(devices, channels // devices, share))
    down_grad = down_rows.transpose(1, 0, 2).reshape(channels // devices, units).astype(F32)
    up_grad = pl.pallas_call(
        up_part_kernel, grid=(devices // group,),
        in_specs=[gathered, gathered, whole((share, channels)), whole((1, share)), whole((channels, share))],
        out_specs=whole((share, channels)), out_shape=struct((share, channels), F32), compiler_params=params,
    )(second_all, cot_all, up_own, bias_own, down_own)
    return (block_output, input_grad, up_grad, down_grad, total[0], total[1])


def solution(mesh):
    tokens = P(("rep", "lat"), None, None)
    return jax.shard_map(
        shards,
        mesh=mesh,
        in_specs=(tokens, tokens) + (P(),) * 12,
        out_specs=(
            tokens,
            tokens,
            P(("rep", "lat"), None),
            P(("rep", "lat"), None),
            P("rep", "lat", None),
            P("rep", "lat", None),
        ),
        check_vma=False,
    )
```

```python
from functools import partial
import math

import jax
import jax.numpy as jnp
import ml_dtypes
import numpy as np
from jax import lax
from jax.experimental import pallas as pl
from jax.experimental.pallas import tpu as pltpu
from jax.sharding import PartitionSpec as P

EPS = 1e-05
SHRINK = 0.01
LANES = 128
BF16 = jnp.bfloat16
F32 = jnp.float32


def dot(a, b, dims=((1,), (0,))):
    return lax.dot_general(a, b, (dims, ((), ())), preferred_element_type=F32)


def split(values):
    high = values.astype(BF16)
    return high, (values - high.astype(F32)).astype(BF16)


def dot3(a, b):
    return dot(a[0], b[0]) + (dot(a[0], b[1]) + dot(a[1], b[0]))


def host_split(table):
    high = table.astype(np.float32).astype(ml_dtypes.bfloat16)
    low = (table - high.astype(np.float64)).astype(np.float32).astype(ml_dtypes.bfloat16)
    return jnp.asarray(np.stack((high, low)))


def lon_table(length, members, per_member, weighted):
    count = length // 2 + 1
    mode = np.arange(members * per_member).reshape(members, 1, per_member, 1)
    angle = 2.0 * np.pi / length * ((mode * np.arange(length)) % length)
    weight = (mode < count) / math.sqrt(length)
    edge = (mode == 0) | (2 * mode == length)
    if weighted:
        weight = weight * np.where(edge, 1.0, 2.0)
    sine = np.where(edge, 0.0, -np.sin(angle))
    table = np.concatenate((np.cos(angle) * weight, sine * weight), axis=1)
    return table.reshape(members * 2 * per_member, length)


def moments(values):
    average = jnp.mean(values, axis=-1, keepdims=True)
    centered = values - average
    variance = jnp.mean(centered * centered, axis=-1, keepdims=True)
    scale = lax.rsqrt(variance + EPS)
    return centered * scale, scale


def norm_grad(unit, scale, grad_unit):
    mean_grad = jnp.mean(grad_unit, axis=-1, keepdims=True)
    mean_dot = jnp.mean(grad_unit * unit, axis=-1, keepdims=True)
    return scale * (grad_unit - mean_grad - unit * mean_dot)


def gelu_and_slope(values):
    magnitude = jnp.abs(values) * math.sqrt(0.5)
    t = 1.0 / (1.0 + 0.3275911 * magnitude)
    bell = jnp.exp(-0.5 * values * values)
    tail = t * (0.127414796 + t * (-0.142248368 + t * (0.7107068705 + t * (-0.7265760135 + t * 0.5307027145))))
    tail = tail * bell
    phi = jnp.where(values < 0.0, tail, 1.0 - tail)
    return values * phi, phi + values * (bell * (1.0 / math.sqrt(2.0 * math.pi)))


def fft(pairs, sign):
    n = len(pairs)
    if n == 1:
        return pairs
    assert n % 2 == 0
    even, odd = fft(pairs[0::2], sign), fft(pairs[1::2], sign)
    low, high = [], []
    for k in range(n // 2):
        (er, ei), (xr, xi) = even[k], odd[k]
        if k == 0:
            tr, ti = xr, xi
        elif 4 * k == n:
            tr, ti = (-xi, xr) if sign > 0 else (xi, -xr)
        else:
            c, s = math.cos(2.0 * math.pi * k / n), sign * math.sin(2.0 * math.pi * k / n)
            tr, ti = xr * c - xi * s, xr * s + xi * c
        low.append((er + tr, ei + ti))
        high.append((er - tr, ei - ti))
    return low + high


def spread(values, block):
    zeros = jnp.zeros((values.shape[0], LANES - block), values.dtype)
    pieces = []
    for b in range(values.shape[1] // block):
        pieces += [jnp.concatenate((values[:, b * block:(b + 1) * block], zeros), axis=1)]
    return jnp.concatenate(pieces, axis=1)


def compact(values, block, blocks):
    return jnp.concatenate([values[:, b * LANES:b * LANES + block] for b in range(blocks)], axis=1)


def lane_mask(shape, low, high):
    lane = lax.broadcasted_iota(jnp.int32, shape, 1)
    return (lane >= low) & (lane < high)


def pack(values, block):
    rows = values.shape[0]
    free = LANES - block
    kept = rows * block // LANES
    spare = rows - kept
    out = []
    for k in range(kept // spare):
        moved = pltpu.roll(values[kept:], block - k * free, 1)
        own = values[k * spare:(k + 1) * spare]
        out.append(jnp.where(lane_mask(own.shape, 0, block), own, moved))
    return jnp.concatenate(out, axis=0)


def unpack(values, block):
    kept = values.shape[0]
    free = LANES - block
    spare = kept * free // block
    last = jnp.zeros((spare, LANES), values.dtype)
    for k in range(kept // spare):
        moved = pltpu.roll(values[k * spare:(k + 1) * spare], LANES - block + k * free, 1)
        last = jnp.where(lane_mask(moved.shape, k * free, (k + 1) * free), moved, last)
    first = jnp.where(lane_mask(values.shape, 0, block), values, 0.0)
    return jnp.concatenate((first, last), axis=0)


def gather_blocks(ref, members, block, out_ref):
    devices = ref.shape[0]
    rows = out_ref.shape[0] // members
    for d in range(devices):
        b, r = d // members, d % members
        out_ref[r * rows:(r + 1) * rows, b * LANES:(b + 1) * LANES] = unpack(ref[d].astype(F32), block).astype(BF16)
    return out_ref[...]


def scatter_blocks(values, members, block, ref):
    rows = values.shape[0] // members
    for d in range(ref.shape[0]):
        b, r = d // members, d % members
        piece = values[r * rows:(r + 1) * rows, b * LANES:(b + 1) * LANES]
        ref[d] = pack(piece, block).astype(BF16)


def pad_rows(values, rows):
    return jnp.concatenate((values, jnp.zeros((rows - values.shape[0], values.shape[1]), values.dtype)), axis=0)


def fetch(pairs, sems):
    copies = [pltpu.make_async_copy(src, dst, sems.at[i]) for i, (src, dst) in enumerate(pairs)]
    for copy in copies:
        copy.start()
    return copies


def first_kernel(members, block, x_hbm, cot_hbm, gain_hbm, shift_hbm, table_hbm, out_ref, pad_ref,
                 x_ref, cot_ref, gain_ref, shift_ref, table_ref, sems):
    copies = fetch(((x_hbm, x_ref), (gain_hbm, gain_ref), (shift_hbm, shift_ref), (table_hbm, table_ref),
                    (cot_hbm, cot_ref)), sems)
    copies[0].wait()
    unit, _ = moments(x_ref[...].astype(F32))
    copies[1].wait()
    copies[2].wait()
    first = unit * gain_ref[...][None] + shift_ref[...][None]
    wide = split(spread(pad_rows(first, pad_ref.shape[0]), block))
    copies[3].wait()
    scatter_blocks(dot3((table_ref[0], table_ref[1]), wide), members, block, out_ref)
    copies[4].wait()
    pad_ref[...] = pad_rows(cot_ref[...].astype(F32), pad_ref.shape[0]).astype(BF16)


def load_transform(ref, block, sign, wide_ref, rows_ref):
    devices, rows, _ = rows_ref.shape
    half = rows // 2
    factor = 1.0 / math.sqrt(devices)
    for h in range(devices):
        rows_ref[h] = unpack(ref[h].astype(F32) * factor, block)
    for row in range(0, half, 8):
        pairs = [(rows_ref[h, row:row + 8], rows_ref[h, half + row:half + row + 8]) for h in range(devices)]
        for h, (re, im) in enumerate(fft(pairs, sign)):
            wide_ref[h * half + row:h * half + row + 8, :LANES] = re
            wide_ref[h * half + row:h * half + row + 8, LANES:] = im


def store_transform(wide_ref, block, sign, ref, rows_ref):
    devices, rows, _ = rows_ref.shape
    half = rows // 2
    factor = 1.0 / math.sqrt(devices)
    for row in range(0, half, 8):
        pairs = [
            (wide_ref[h * half + row:h * half + row + 8, :LANES], wide_ref[h * half + row:h * half + row + 8, LANES:])
            for h in range(devices)
        ]
        for h, (re, im) in enumerate(fft(pairs, sign)):
            rows_ref[h, row:row + 8] = re
            rows_ref[h, half + row:half + row + 8] = im
    for h in range(devices):
        ref[h] = (pack(rows_ref[h], block) * factor).astype(BF16)


def filter_kernel(block, in_ref, w1_ref, b1_ref, w2_ref, b2_ref,
                  out_ref, spec_hbm, hid_hbm, slope_hbm, shrink_hbm, wide_ref, rows_ref,
                  spec_ref, hid_ref, slope_ref, shrink_ref, sems):
    def keep(which, ref, hbm):
        copy = pltpu.make_async_copy(ref, hbm, sems.at[which])
        copy.start()
        return copy

    load_transform(in_ref, block, -1.0, wide_ref, rows_ref)
    spectrum = split(wide_ref[...])
    spec_ref[...] = spectrum[0]
    copies = [keep(0, spec_ref, spec_hbm)]
    pre = dot3(spectrum, split(w1_ref[...])) + b1_ref[...]
    inner, slope = gelu_and_slope(pre)
    slope_ref[...] = slope.astype(BF16)
    inner = split(inner)
    hid_ref[...] = inner[0]
    copies += [keep(1, hid_ref, hid_hbm), keep(2, slope_ref, slope_hbm)]
    outer = dot3(inner, split(w2_ref[...])) + b2_ref[...]
    bend = jnp.tanh(outer / SHRINK)
    shrink_ref[...] = (bend * bend).astype(BF16)
    copies += [keep(3, shrink_ref, shrink_hbm)]
    wide_ref[...] = outer - SHRINK * bend
    store_transform(wide_ref, block, 1.0, out_ref, rows_ref)
    for copy in copies:
        copy.wait()


def complex_grad(grad, block):
    a, b = slice(0, block), slice(LANES, LANES + block)
    return grad[a, a] + grad[b, b], grad[a, b] - grad[b, a]


def filter_grad_kernel(block, in_ref, w1_ref, w2_ref, spec_hbm, hid_hbm, slope_hbm, shrink_hbm,
                       out_ref, grads_ref, wide_ref, rows_ref, spec_ref, hid_ref, slope_ref, shrink_ref, sems):
    copies = fetch(((shrink_hbm, shrink_ref), (slope_hbm, slope_ref), (spec_hbm, spec_ref), (hid_hbm, hid_ref)), sems)
    load_transform(in_ref, block, -1.0, wide_ref, rows_ref)
    copies[0].wait()
    grad_outer = (wide_ref[...] * shrink_ref[...].astype(F32)).astype(BF16)
    grad_inner = dot(grad_outer, w2_ref[...].astype(BF16), ((1,), (1,)))
    copies[1].wait()
    grad_pre = (grad_inner * slope_ref[...].astype(F32)).astype(BF16)
    wide_ref[...] = dot(grad_pre, w1_ref[...].astype(BF16), ((1,), (1,)))
    store_transform(wide_ref, block, 1.0, out_ref, rows_ref)
    copies[2].wait()
    re, im = complex_grad(dot(spec_ref[...], grad_pre, ((0,), (0,))), block)
    grads_ref[0, 0] = re
    grads_ref[0, 1] = im
    copies[3].wait()
    re, im = complex_grad(dot(hid_ref[...], grad_outer, ((0,), (0,))), block)
    grads_ref[1, 0] = re
    grads_ref[1, 1] = im


def second_kernel(members, block, blocks, in_ref, x_hbm, gain1_hbm, shift1_hbm, gain2_hbm, shift2_hbm, table_hbm,
                  resid_ref, second_ref, rows_ref, table_ref, x_ref, gain1_ref, shift1_ref, gain2_ref, shift2_ref,
                  sems):
    copies = fetch(((x_hbm, x_ref), (gain1_hbm, gain1_ref), (shift1_hbm, shift1_ref), (table_hbm, table_ref),
                    (gain2_hbm, gain2_ref), (shift2_hbm, shift2_ref)), sems)
    back = gather_blocks(in_ref, members, block, rows_ref)
    for copy in copies[:3]:
        copy.wait()
    x = x_ref[...].astype(F32)
    unit, _ = moments(x)
    x = pad_rows(x + (unit * gain1_ref[...][None] + shift1_ref[...][None]), resid_ref.shape[0])
    for copy in copies[3:]:
        copy.wait()
    filtered = compact(dot(table_ref[0], back) + dot(table_ref[1], back), block, blocks)
    residual = (x + filtered).astype(BF16)
    resid_ref[...] = residual
    unit, _ = moments(residual.astype(F32))
    second = unit * gain2_ref[...][None] + shift2_ref[...][None]
    second_ref[...] = pad_rows(second[:x_ref.shape[0]], resid_ref.shape[0]).astype(BF16)


def mlp_kernel(members, block, chunk, second_ref, resid_hbm, cot_hbm, gain_hbm, up_hbm, upb_hbm, ghid_hbm, table_hbm,
               hid_ref, gres_ref, out_ref, acc_ref, resid_ref, cot_ref, gain_ref, up_ref, upb_ref, ghid_ref, table_ref,
               sems):
    units = up_ref.shape[0]
    parts = [slice(start, start + chunk) for start in range(0, units, chunk)]
    pairs = [(upb_hbm, upb_ref)]
    for part in parts:
        pairs += [(up_hbm.at[part], up_ref.at[part]), (ghid_hbm.at[:, part], ghid_ref.at[:, part])]
    tail = len(pairs)
    pairs += [(resid_hbm, resid_ref), (cot_hbm, cot_ref), (gain_hbm, gain_ref), (table_hbm, table_ref)]
    copies = fetch(pairs, sems)
    copies[0].wait()
    for i, part in enumerate(parts):
        copies[2 * i + 1].wait()
        pre = dot(second_ref[...], up_ref[part], ((1,), (1,))) + upb_ref[:, part]
        hidden, slope = gelu_and_slope(pre)
        hid_ref[:, part] = hidden.astype(BF16)
        copies[2 * i + 2].wait()
        grad_pre = (ghid_ref[:, part] * slope).astype(BF16)
        term = dot(grad_pre, up_ref[part])
        if i == 0:
            acc_ref[...] = term
        else:
            acc_ref[...] += term
    for copy in copies[tail:]:
        copy.wait()
    unit, scale = moments(resid_ref[...].astype(F32))
    grad = cot_ref[...].astype(F32) + norm_grad(unit, scale, acc_ref[...] * gain_ref[...][None])
    gres_ref[...] = grad
    wide = split(spread(grad, block))
    scatter_blocks(dot3((table_ref[0], table_ref[1]), wide), members, block, out_ref)


def last_kernel(members, block, blocks, in_ref, x_hbm, gain_hbm, gres_hbm, table_hbm, out_ref, rows_ref, table_ref,
                x_ref, gain_ref, gres_ref, sems):
    copies = fetch(((x_hbm, x_ref), (gain_hbm, gain_ref), (gres_hbm, gres_ref), (table_hbm, table_ref)), sems)
    back = gather_blocks(in_ref, members, block, rows_ref)
    for copy in copies:
        copy.wait()
    unit, scale = moments(x_ref[...].astype(F32))
    length = unit.shape[0]
    gres = gres_ref[:length]
    grad = compact(dot(table_ref[0], back) + dot(table_ref[1], back), block, blocks)[:length]
    out_ref[...] = (gres + norm_grad(unit, scale, (grad + gres) * gain_ref[...][None])).astype(BF16)


def down_part_kernel(second_ref, cot_ref, up_ref, bias_ref, out_ref, acc_ref):
    step = pl.program_id(0)
    tokens = second_ref.shape[0] * second_ref.shape[1]
    second = second_ref[...].reshape(tokens, -1)
    hidden, _ = gelu_and_slope(dot(up_ref[...], second, ((1,), (1,))) + bias_ref[...])
    term = dot(hidden.astype(BF16), cot_ref[...].reshape(tokens, -1))

    @pl.when(step == 0)
    def _():
        acc_ref[...] = term

    @pl.when(step > 0)
    def _():
        acc_ref[...] += term

    @pl.when(step == pl.num_programs(0) - 1)
    def _():
        out_ref[...] = acc_ref[...].T.astype(BF16)


def up_part_kernel(second_ref, cot_ref, up_ref, bias_ref, down_ref, out_ref):
    step = pl.program_id(0)
    tokens = second_ref.shape[0] * second_ref.shape[1]
    second = second_ref[...].reshape(tokens, -1)
    _, slope = gelu_and_slope(dot(up_ref[...], second, ((1,), (1,))) + bias_ref[...])
    grad_hidden = dot(down_ref[...], cot_ref[...].reshape(tokens, -1), ((1,), (1,)))
    term = dot((grad_hidden * slope).astype(BF16), second)

    @pl.when(step == 0)
    def _():
        out_ref[...] = term

    @pl.when(step > 0)
    def _():
        out_ref[...] += term


def struct(shape, dtype):
    return jax.ShapeDtypeStruct(shape, dtype)


VMEM = pl.BlockSpec(memory_space=pltpu.VMEM)
HBM = pl.BlockSpec(memory_space=pltpu.HBM)


def call(kernel, out, scratch, in_specs, *args, out_specs=None, limit=24):
    if out_specs is None:
        out_specs = jax.tree.map(lambda _: VMEM, out)
    args = [pltpu.with_memory_space_constraint(a, pltpu.HBM) if spec is HBM else a for a, spec in zip(args, in_specs)]
    return pl.pallas_call(
        kernel, out_shape=out, scratch_shapes=scratch, in_specs=in_specs, out_specs=out_specs,
        compiler_params=pltpu.CompilerParams(vmem_limit_bytes=limit << 20))(*args)


def ring_order(devices):
    width = devices // 8
    chips = []
    for row in range(4):
        columns = list(range(1, width))
        chips += [row * width + c for c in (columns if row % 2 == 0 else columns[::-1])]
    chips += [row * width for row in (3, 2, 1, 0)]
    return [2 * chip + core for chip in chips for core in (0, 1)]


def complex_weight(weight, block):
    pad = ((0, LANES - block), (0, LANES - block))
    re, im = jnp.pad(weight[0], pad), jnp.pad(weight[1], pad)
    return jnp.concatenate((jnp.concatenate((re, im), 1), jnp.concatenate((-im, re), 1)), 0)


def shards(
    block_input,
    cotangent,
    first_gain,
    first_shift,
    inner_weight,
    inner_bias,
    outer_weight,
    outer_bias,
    second_gain,
    second_shift,
    up_weight,
    up_bias,
    down_weight,
    down_bias,
):
    bands, length, channels = block_input.shape
    assert bands == 1
    devices = lax.axis_size("lat")
    index = lax.axis_index("lat")
    block = inner_weight.shape[2]
    blocks = channels // block
    members = devices // blocks
    per_member = -(-(length // 2 + 1) // members)
    per_member = -(-per_member // 16) * 16
    rows = 2 * per_member
    units = up_weight.shape[0]
    tokens = -(-length // 64) * 64
    x = block_input[0]
    ring = [ring_order(devices)]
    all_gather = partial(lax.all_gather, axis_name="lat", axis=0, axis_index_groups=ring)
    a2a = partial(lax.all_to_all, axis_name="lat", split_axis=0, concat_axis=0, tiled=True)

    fwd = np.pad(lon_table(length, members, per_member, False), ((0, 0), (0, tokens - length)))
    inv = np.pad(lon_table(length, members, per_member, True), ((0, 0), (0, tokens - length)))
    all_rows, wide = members * rows, blocks * LANES
    packed = struct((devices, rows * block // LANES, LANES), BF16)
    row_scratch = pltpu.VMEM((all_rows, wide), BF16)
    table_scratch = pltpu.VMEM((2, all_rows, tokens), BF16)
    back_scratch = pltpu.VMEM((2, tokens, all_rows), BF16)
    sems = lambda count: pltpu.SemaphoreType.DMA((count,))
    row = pltpu.VMEM((channels,), F32)
    short = pltpu.VMEM((length, channels), BF16)

    start = (index // members) * block
    def own(array):
        return lax.dynamic_slice_in_dim(array, start, block, 1)
    w1 = complex_weight(own(inner_weight), block)
    w2 = complex_weight(own(outer_weight), block)
    b1 = jnp.pad(own(inner_bias), ((0, 0), (0, LANES - block))).reshape(1, 2 * LANES)
    b2 = jnp.pad(own(outer_bias), ((0, 0), (0, LANES - block))).reshape(1, 2 * LANES)

    token = struct((tokens, channels), BF16)
    outgoing, cot = call(
        partial(first_kernel, members, block), (packed, token), [short, short, row, row, table_scratch, sems(5)],
        [HBM] * 5, x, cotangent[0], first_gain, first_shift, host_split(fwd))
    cot_all = all_gather(cot)
    incoming = a2a(outgoing)
    grad_hidden = dot(cot, down_weight)
    spectral = struct((devices * per_member, 2 * LANES), BF16)
    kept_scratch = [pltpu.VMEM(spectral.shape, BF16)] * 4 + [sems(4)]
    spectral_scratch = [pltpu.VMEM(spectral.shape, F32), pltpu.VMEM((devices, rows, LANES), F32)] + kept_scratch
    returning, *kept = call(
        partial(filter_kernel, block), (packed, spectral, spectral, spectral, spectral), spectral_scratch,
        [VMEM] * 5, incoming, w1, b1, w2, b2, out_specs=(VMEM, HBM, HBM, HBM, HBM))
    back, grad_hidden = lax.optimization_barrier((a2a(returning), grad_hidden))
    residual, second = call(
        partial(second_kernel, members, block, blocks), (token, token),
        [row_scratch, back_scratch, short, row, row, row, row, sems(6)], [VMEM] + [HBM] * 6,
        back, x, first_gain, first_shift, second_gain, second_shift, host_split(inv.T))
    second_out, cot_all = lax.optimization_barrier((second, cot_all))
    second_all = all_gather(second_out)

    chunk = 512
    full = pltpu.VMEM((tokens, channels), BF16)
    hidden, grad_resid, grad_out = call(
        partial(mlp_kernel, members, block, chunk),
        (struct((tokens, units), BF16), struct((tokens, channels), F32), packed),
        [pltpu.VMEM((tokens, channels), F32), full, full, row, pltpu.VMEM((units, channels), BF16),
         pltpu.VMEM((1, units), F32), pltpu.VMEM((tokens, units), F32), table_scratch,
         sems(2 * (units // chunk) + 5)],
        [VMEM] + [HBM] * 7,
        second, residual, cot, second_gain, up_weight, up_bias[None], grad_hidden, host_split(inv), limit=32)
    grad_in = a2a(grad_out)
    block_output = (
        residual.astype(F32) + dot(hidden, down_weight, ((1,), (1,))) + down_bias
    ).astype(BF16)[None, :length]

    grad_back, terms = call(
        partial(filter_grad_kernel, block), (packed, struct((2, 2, block, block), F32)), spectral_scratch,
        [VMEM] * 3 + [HBM] * 4, grad_in, w1, w2, *kept)
    grad_lon = a2a(grad_back)
    input_grad = call(
        partial(last_kernel, members, block, blocks), struct((length, channels), BF16),
        [row_scratch, back_scratch, short, row, pltpu.VMEM((tokens, channels), F32), sems(4)], [VMEM] + [HBM] * 4,
        grad_lon, x, first_gain, grad_resid, host_split(fwd.T))[None]

    part = block // members
    terms = terms.reshape(2, 2, members, part, block)
    member = index % members
    def piece(which):
        return lax.dynamic_index_in_dim(terms, which, 2, keepdims=False)
    total = piece(member)
    for hop in range(1, members):
        pairs = [(d, d - d % members + (d % members + hop) % members) for d in range(devices)]
        total = total + lax.ppermute(piece((member + hop) % members), "lat", pairs)

    share = units // devices
    up_own = lax.dynamic_slice_in_dim(up_weight, index * share, share, 0)
    bias_own = lax.dynamic_slice_in_dim(up_bias, index * share, share, 0)[:, None]
    down_own = lax.dynamic_slice_in_dim(down_weight, index * share, share, 1).T
    group = 4 if devices % 4 == 0 else 1
    whole = lambda shape: pl.BlockSpec(shape, lambda i: (0,) * len(shape))
    gathered = pl.BlockSpec((group, tokens, channels), lambda i: (i, 0, 0))
    params = pltpu.CompilerParams(vmem_limit_bytes=24 << 20)
    gathered_pair = [pltpu.with_memory_space_constraint(array, pltpu.HBM) for array in (second_all, cot_all)]
    down_part = pl.pallas_call(
        down_part_kernel, grid=(devices // group,),
        in_specs=[gathered, gathered, whole((share, channels)), whole((share, 1))],
        out_specs=whole((channels, share)), out_shape=struct((channels, share), BF16),
        scratch_shapes=[pltpu.VMEM((share, channels), F32)], compiler_params=params,
    )(*gathered_pair, up_own, bias_own)
    down_rows = a2a(down_part.reshape(devices, channels // devices, share))
    down_grad = down_rows.transpose(1, 0, 2).reshape(channels // devices, units).astype(F32)
    up_grad = pl.pallas_call(
        up_part_kernel, grid=(devices // group,),
        in_specs=[gathered, gathered, whole((share, channels)), whole((share, 1)), whole((share, channels))],
        out_specs=whole((share, channels)), out_shape=struct((share, channels), F32), compiler_params=params,
    )(*gathered_pair, up_own, bias_own, down_own)
    return (block_output, input_grad, up_grad, down_grad, total[0], total[1])


def solution(mesh):
    tokens = P(("rep", "lat"), None, None)
    return jax.shard_map(
        shards,
        mesh=mesh,
        in_specs=(tokens, tokens) + (P(),) * 12,
        out_specs=(
            tokens,
            tokens,
            P(("rep", "lat"), None),
            P(("rep", "lat"), None),
            P("rep", "lat", None),
            P("rep", "lat", None),
        ),
        check_vma=False,
    )
```

```python
from functools import partial
import math

import jax
import jax.numpy as jnp
import ml_dtypes
import numpy as np
from jax import lax
from jax.experimental import pallas as pl
from jax.experimental.pallas import tpu as pltpu
from jax.sharding import PartitionSpec as P

EPS = 1e-05
SHRINK = 0.01
LANES = 128
BF16 = jnp.bfloat16
F32 = jnp.float32


def dot(a, b, dims=((1,), (0,))):
    return lax.dot_general(a, b, (dims, ((), ())), preferred_element_type=F32)


def split(values):
    high = values.astype(BF16)
    return high, (values - high.astype(F32)).astype(BF16)


def dot3(a, b):
    return dot(a[0], b[0]) + (dot(a[0], b[1]) + dot(a[1], b[0]))


def host_split(table):
    high = table.astype(np.float32).astype(ml_dtypes.bfloat16)
    low = (table - high.astype(np.float64)).astype(np.float32).astype(ml_dtypes.bfloat16)
    return jnp.asarray(np.stack((high, low)))


def lon_table(length, members, per_member, weighted):
    count = length // 2 + 1
    mode = np.arange(members * per_member).reshape(members, 1, per_member, 1)
    angle = 2.0 * np.pi / length * ((mode * np.arange(length)) % length)
    weight = (mode < count) / math.sqrt(length)
    edge = (mode == 0) | (2 * mode == length)
    if weighted:
        weight = weight * np.where(edge, 1.0, 2.0)
    sine = np.where(edge, 0.0, -np.sin(angle))
    table = np.concatenate((np.cos(angle) * weight, sine * weight), axis=1)
    return table.reshape(members * 2 * per_member, length)


def moments(values):
    average = jnp.mean(values, axis=-1, keepdims=True)
    centered = values - average
    variance = jnp.mean(centered * centered, axis=-1, keepdims=True)
    scale = lax.rsqrt(variance + EPS)
    return centered * scale, scale


def norm_grad(unit, scale, grad_unit):
    mean_grad = jnp.mean(grad_unit, axis=-1, keepdims=True)
    mean_dot = jnp.mean(grad_unit * unit, axis=-1, keepdims=True)
    return scale * (grad_unit - mean_grad - unit * mean_dot)


def gelu_and_slope(values):
    magnitude = jnp.abs(values) * math.sqrt(0.5)
    t = 1.0 / (1.0 + 0.3275911 * magnitude)
    bell = jnp.exp(-0.5 * values * values)
    tail = t * (0.127414796 + t * (-0.142248368 + t * (0.7107068705 + t * (-0.7265760135 + t * 0.5307027145))))
    tail = tail * bell
    phi = jnp.where(values < 0.0, tail, 1.0 - tail)
    return values * phi, phi + values * (bell * (1.0 / math.sqrt(2.0 * math.pi)))


def fft(pairs, sign):
    n = len(pairs)
    if n == 1:
        return pairs
    assert n % 2 == 0
    even, odd = fft(pairs[0::2], sign), fft(pairs[1::2], sign)
    low, high = [], []
    for k in range(n // 2):
        (er, ei), (xr, xi) = even[k], odd[k]
        if k == 0:
            tr, ti = xr, xi
        elif 4 * k == n:
            tr, ti = (-xi, xr) if sign > 0 else (xi, -xr)
        else:
            c, s = math.cos(2.0 * math.pi * k / n), sign * math.sin(2.0 * math.pi * k / n)
            tr, ti = xr * c - xi * s, xr * s + xi * c
        low.append((er + tr, ei + ti))
        high.append((er - tr, ei - ti))
    return low + high


def spread(values, block):
    zeros = jnp.zeros((values.shape[0], LANES - block), values.dtype)
    pieces = []
    for b in range(values.shape[1] // block):
        pieces += [jnp.concatenate((values[:, b * block:(b + 1) * block], zeros), axis=1)]
    return jnp.concatenate(pieces, axis=1)


def compact(values, block, blocks):
    return jnp.concatenate([values[:, b * LANES:b * LANES + block] for b in range(blocks)], axis=1)


def lane_mask(shape, low, high):
    lane = lax.broadcasted_iota(jnp.int32, shape, 1)
    return (lane >= low) & (lane < high)


def pack(values, block):
    rows = values.shape[0]
    free = LANES - block
    kept = rows * block // LANES
    spare = rows - kept
    out = []
    for k in range(kept // spare):
        moved = pltpu.roll(values[kept:], block - k * free, 1)
        own = values[k * spare:(k + 1) * spare]
        out.append(jnp.where(lane_mask(own.shape, 0, block), own, moved))
    return jnp.concatenate(out, axis=0)


def unpack(values, block):
    kept = values.shape[0]
    free = LANES - block
    spare = kept * free // block
    last = jnp.zeros((spare, LANES), values.dtype)
    for k in range(kept // spare):
        moved = pltpu.roll(values[k * spare:(k + 1) * spare], LANES - block + k * free, 1)
        last = jnp.where(lane_mask(moved.shape, k * free, (k + 1) * free), moved, last)
    first = jnp.where(lane_mask(values.shape, 0, block), values, 0.0)
    return jnp.concatenate((first, last), axis=0)


def gather_blocks(ref, members, block, out_ref):
    devices = ref.shape[0]
    rows = out_ref.shape[0] // members
    for d in range(devices):
        b, r = d // members, d % members
        out_ref[r * rows:(r + 1) * rows, b * LANES:(b + 1) * LANES] = unpack(ref[d].astype(F32), block).astype(BF16)
    return out_ref[...]


def scatter_blocks(values, members, block, ref):
    rows = values.shape[0] // members
    for d in range(ref.shape[0]):
        b, r = d // members, d % members
        piece = values[r * rows:(r + 1) * rows, b * LANES:(b + 1) * LANES]
        ref[d] = pack(piece, block).astype(BF16)


def pad_rows(values, rows):
    return jnp.concatenate((values, jnp.zeros((rows - values.shape[0], values.shape[1]), values.dtype)), axis=0)


def fetch(pairs, sems):
    copies = [pltpu.make_async_copy(src, dst, sems.at[i]) for i, (src, dst) in enumerate(pairs)]
    for copy in copies:
        copy.start()
    return copies


def first_kernel(members, block, x_hbm, cot_hbm, gain_hbm, shift_hbm, table_hbm, out_ref, pad_ref,
                 x_ref, cot_ref, gain_ref, shift_ref, table_ref, sems):
    copies = fetch(((x_hbm, x_ref), (gain_hbm, gain_ref), (shift_hbm, shift_ref), (table_hbm, table_ref),
                    (cot_hbm, cot_ref)), sems)
    copies[0].wait()
    unit, _ = moments(x_ref[...].astype(F32))
    copies[1].wait()
    copies[2].wait()
    first = unit * gain_ref[...][None] + shift_ref[...][None]
    wide = split(spread(pad_rows(first, pad_ref.shape[0]), block))
    copies[3].wait()
    scatter_blocks(dot3((table_ref[0], table_ref[1]), wide), members, block, out_ref)
    copies[4].wait()
    pad_ref[...] = pad_rows(cot_ref[...].astype(F32), pad_ref.shape[0]).astype(BF16)


def load_transform(ref, block, sign, wide_ref, rows_ref):
    devices, rows, _ = rows_ref.shape
    half = rows // 2
    factor = 1.0 / math.sqrt(devices)
    for h in range(devices):
        rows_ref[h] = unpack(ref[h].astype(F32) * factor, block)
    for row in range(0, half, 8):
        pairs = [(rows_ref[h, row:row + 8], rows_ref[h, half + row:half + row + 8]) for h in range(devices)]
        for h, (re, im) in enumerate(fft(pairs, sign)):
            wide_ref[h * half + row:h * half + row + 8, :LANES] = re
            wide_ref[h * half + row:h * half + row + 8, LANES:] = im


def store_transform(wide_ref, block, sign, ref, rows_ref):
    devices, rows, _ = rows_ref.shape
    half = rows // 2
    factor = 1.0 / math.sqrt(devices)
    for row in range(0, half, 8):
        pairs = [
            (wide_ref[h * half + row:h * half + row + 8, :LANES], wide_ref[h * half + row:h * half + row + 8, LANES:])
            for h in range(devices)
        ]
        for h, (re, im) in enumerate(fft(pairs, sign)):
            rows_ref[h, row:row + 8] = re
            rows_ref[h, half + row:half + row + 8] = im
    for h in range(devices):
        ref[h] = (pack(rows_ref[h], block) * factor).astype(BF16)


def filter_kernel(block, in_ref, w1_ref, b1_ref, w2_ref, b2_ref,
                  out_ref, spec_hbm, hid_hbm, slope_hbm, shrink_hbm, wide_ref, rows_ref,
                  spec_ref, hid_ref, slope_ref, shrink_ref, sems):
    def keep(which, ref, hbm):
        copy = pltpu.make_async_copy(ref, hbm, sems.at[which])
        copy.start()
        return copy

    load_transform(in_ref, block, -1.0, wide_ref, rows_ref)
    spectrum = split(wide_ref[...])
    spec_ref[...] = spectrum[0]
    copies = [keep(0, spec_ref, spec_hbm)]
    pre = dot3(spectrum, split(w1_ref[...])) + b1_ref[...]
    inner, slope = gelu_and_slope(pre)
    slope_ref[...] = slope.astype(BF16)
    inner = split(inner)
    hid_ref[...] = inner[0]
    copies += [keep(1, hid_ref, hid_hbm), keep(2, slope_ref, slope_hbm)]
    outer = dot3(inner, split(w2_ref[...])) + b2_ref[...]
    bend = jnp.tanh(outer / SHRINK)
    shrink_ref[...] = (bend * bend).astype(BF16)
    copies += [keep(3, shrink_ref, shrink_hbm)]
    wide_ref[...] = outer - SHRINK * bend
    store_transform(wide_ref, block, 1.0, out_ref, rows_ref)
    for copy in copies:
        copy.wait()


def complex_grad(grad, block):
    a, b = slice(0, block), slice(LANES, LANES + block)
    return grad[a, a] + grad[b, b], grad[a, b] - grad[b, a]


def filter_grad_kernel(block, in_ref, w1_ref, w2_ref, spec_hbm, hid_hbm, slope_hbm, shrink_hbm,
                       out_ref, grads_ref, wide_ref, rows_ref, spec_ref, hid_ref, slope_ref, shrink_ref, sems):
    copies = fetch(((shrink_hbm, shrink_ref), (slope_hbm, slope_ref), (spec_hbm, spec_ref), (hid_hbm, hid_ref)), sems)
    load_transform(in_ref, block, -1.0, wide_ref, rows_ref)
    copies[0].wait()
    grad_outer = (wide_ref[...] * shrink_ref[...].astype(F32)).astype(BF16)
    grad_inner = dot(grad_outer, w2_ref[...].astype(BF16), ((1,), (1,)))
    copies[1].wait()
    grad_pre = (grad_inner * slope_ref[...].astype(F32)).astype(BF16)
    wide_ref[...] = dot(grad_pre, w1_ref[...].astype(BF16), ((1,), (1,)))
    store_transform(wide_ref, block, 1.0, out_ref, rows_ref)
    copies[2].wait()
    re, im = complex_grad(dot(spec_ref[...], grad_pre, ((0,), (0,))), block)
    grads_ref[0, 0] = re
    grads_ref[0, 1] = im
    copies[3].wait()
    re, im = complex_grad(dot(hid_ref[...], grad_outer, ((0,), (0,))), block)
    grads_ref[1, 0] = re
    grads_ref[1, 1] = im


def second_kernel(members, block, blocks, in_hbm, x_hbm, gain1_hbm, shift1_hbm, gain2_hbm, shift2_hbm, table_hbm,
                  up_hbm, resid_ref, second_ref, up_ref, in_ref, rows_ref, table_ref, x_ref, gain1_ref, shift1_ref, gain2_ref, shift2_ref,
                  sems):
    copies = fetch(((x_hbm, x_ref), (gain1_hbm, gain1_ref), (shift1_hbm, shift1_ref), (table_hbm, table_ref),
                    (gain2_hbm, gain2_ref), (shift2_hbm, shift2_ref), (in_hbm, in_ref), (up_hbm, up_ref)), sems)
    copies[6].wait()
    back = gather_blocks(in_ref, members, block, rows_ref)
    for copy in copies[:3]:
        copy.wait()
    x = x_ref[...].astype(F32)
    unit, _ = moments(x)
    x = pad_rows(x + (unit * gain1_ref[...][None] + shift1_ref[...][None]), resid_ref.shape[0])
    for copy in copies[3:6]:
        copy.wait()
    filtered = compact(dot(table_ref[0], back) + dot(table_ref[1], back), block, blocks)
    residual = (x + filtered).astype(BF16)
    resid_ref[...] = residual
    unit, _ = moments(residual.astype(F32))
    second = unit * gain2_ref[...][None] + shift2_ref[...][None]
    second_ref[...] = pad_rows(second[:x_ref.shape[0]], resid_ref.shape[0]).astype(BF16)
    copies[7].wait()


def prepare_kernel(cot_hbm, down_hbm, ghid_ref, cot_ref, down_ref, sems):
    for copy in fetch(((cot_hbm, cot_ref), (down_hbm, down_ref)), sems):
        copy.wait()
    ghid_ref[...] = dot(cot_ref[...], down_ref[...])


def mlp_kernel(members, block, chunk, second_ref, up_ref, ghid_ref, resid_hbm, cot_hbm, gain_hbm, upb_hbm, table_hbm,
               hid_hbm, gres_hbm, out_ref, acc_ref, hid_ref, gres_ref, resid_ref, cot_ref, gain_ref, upb_ref, table_ref,
               sems):
    copies = fetch(((upb_hbm, upb_ref), (resid_hbm, resid_ref), (cot_hbm, cot_ref), (gain_hbm, gain_ref),
                    (table_hbm, table_ref)), sems)
    copies[0].wait()
    for start in range(0, up_ref.shape[0], chunk):
        part = slice(start, start + chunk)
        pre = dot(second_ref[...], up_ref[part], ((1,), (1,))) + upb_ref[:, part]
        hidden, slope = gelu_and_slope(pre)
        hid_ref[:, part] = hidden.astype(BF16)
        grad_pre = (ghid_ref[:, part] * slope).astype(BF16)
        term = dot(grad_pre, up_ref[part])
        if start == 0:
            acc_ref[...] = term
        else:
            acc_ref[...] += term
    hid_copy = pltpu.make_async_copy(hid_ref, hid_hbm, sems.at[5])
    hid_copy.start()
    for copy in copies[1:]:
        copy.wait()
    unit, scale = moments(resid_ref[...].astype(F32))
    grad = cot_ref[...].astype(F32) + norm_grad(unit, scale, acc_ref[...] * gain_ref[...][None])
    gres_ref[...] = grad
    gres_copy = pltpu.make_async_copy(gres_ref, gres_hbm, sems.at[6])
    gres_copy.start()
    wide = split(spread(grad, block))
    scatter_blocks(dot3((table_ref[0], table_ref[1]), wide), members, block, out_ref)
    hid_copy.wait()
    gres_copy.wait()


def last_kernel(members, block, blocks, in_ref, x_hbm, gain_hbm, gres_hbm, table_hbm, out_ref, rows_ref, table_ref,
                x_ref, gain_ref, gres_ref, sems):
    copies = fetch(((x_hbm, x_ref), (gain_hbm, gain_ref), (gres_hbm, gres_ref), (table_hbm, table_ref)), sems)
    back = gather_blocks(in_ref, members, block, rows_ref)
    for copy in copies:
        copy.wait()
    unit, scale = moments(x_ref[...].astype(F32))
    length = unit.shape[0]
    gres = gres_ref[:length]
    grad = compact(dot(table_ref[0], back) + dot(table_ref[1], back), block, blocks)[:length]
    out_ref[...] = (gres + norm_grad(unit, scale, (grad + gres) * gain_ref[...][None])).astype(BF16)


def token_chunks(ref, width=384):
    tokens = ref.shape[0]
    return [slice(start, min(start + width, tokens)) for start in range(0, tokens, width)]


def fetch_blocks(blocks, ref, sems, base):
    size = ref.shape[0] // len(blocks)
    copies = []
    for i, block in enumerate(blocks):
        copy = pltpu.make_async_copy(block, ref.at[i * size:(i + 1) * size], sems.at[base + i])
        copy.start()
        copies += [copy]
    return copies


def wait_blocks(copies, part, size):
    for i in range(part.start // size, part.stop // size):
        copies[i].wait()


def grads_kernel(count, has_terms, spill, *refs):
    refs = list(refs)
    take = lambda n: [refs.pop(0) for _ in range(n)]
    seconds, cots = take(count), take(count)
    up_ref, bias_ref, down_ref, _ = take(4)
    terms = take(2 * has_terms)
    outs = take(2)
    second_ref, cot_ref, sums_ref, sems = take(4)
    size = second_ref.shape[0] // count
    second_copies = fetch_blocks(seconds, second_ref, sems, 0)
    cot_copies = fetch_blocks(cots, cot_ref, sems, count)
    term_copies = [
        pltpu.make_async_copy(term, sums_ref.at[i], sems.at[2 * count + i]) for i, term in enumerate(terms)]
    for copy in term_copies:
        copy.start()
    sums = [0.0, 0.0]
    for part in token_chunks(second_ref):
        wait_blocks(second_copies, part, size)
        hidden, slope = gelu_and_slope(dot(up_ref[...], second_ref[part], ((1,), (1,))) + bias_ref[...])
        wait_blocks(cot_copies, part, size)
        sums[0] = sums[0] + dot(hidden.astype(BF16), cot_ref[part])
        grad_hidden = dot(down_ref[...], cot_ref[part], ((1,), (1,)))
        sums[1] = sums[1] + dot((grad_hidden * slope).astype(BF16), second_ref[part])
    for copy in term_copies:
        copy.wait()
    half = sums[0].shape[0] // 2
    out_copies = []
    for i, (out, total) in enumerate(zip(outs, sums)):
        if has_terms:
            total = total + jnp.concatenate((sums_ref[i, 0], sums_ref[i, 1]), axis=0)
        target = sums_ref.at[i] if spill else out
        target[0] = total[:half]
        target[1] = total[half:]
        if spill:
            out_copies += [pltpu.make_async_copy(sums_ref.at[i], out, sems.at[2 * count + i])]
            out_copies[-1].start()
    for copy in out_copies:
        copy.wait()


def join_kernel(in_ref, out_ref):
    width = in_ref.shape[2]
    for d in range(in_ref.shape[0]):
        out_ref[:, d * width:(d + 1) * width] = in_ref[d].astype(F32)


def turn_kernel(own_ref, other_ref, out_ref):
    out_ref[...] = (own_ref[...] + other_ref[...]).T.astype(BF16)


def struct(shape, dtype):
    return jax.ShapeDtypeStruct(shape, dtype)


VMEM = pl.BlockSpec(memory_space=pltpu.VMEM)
PINNED = pl.BlockSpec(memory_space=pltpu.VMEM)
HBM = pl.BlockSpec(memory_space=pltpu.HBM)
EITHER = pl.BlockSpec(memory_space=pl.ANY)


def call(kernel, out, scratch, in_specs, *args, out_specs=None, limit=12, cost=1):
    if out_specs is None:
        out_specs = jax.tree.map(lambda _: VMEM, out)
    flat = out_specs if isinstance(out_specs, tuple) else (out_specs,)
    shapes = out if isinstance(out, tuple) else (out,)
    shapes = tuple(
        pltpu.HBM(o.shape, o.dtype) if spec is HBM else pltpu.VMEM(o.shape, o.dtype) if spec is PINNED else o
        for o, spec in zip(shapes, flat))
    out = shapes if isinstance(out, tuple) else shapes[0]
    spaces = {id(HBM): pltpu.HBM, id(PINNED): pltpu.VMEM}
    args = [
        pltpu.with_memory_space_constraint(a, spaces[id(spec)]) if id(spec) in spaces else a
        for a, spec in zip(args, in_specs)]
    return pl.pallas_call(
        kernel, out_shape=out, scratch_shapes=scratch, in_specs=in_specs, out_specs=out_specs,
        cost_estimate=pl.CostEstimate(flops=cost, transcendentals=0, bytes_accessed=cost),
        compiler_params=pltpu.CompilerParams(vmem_limit_bytes=limit << 20))(*args)


def ring_order(devices):
    width = devices // 8
    chips = []
    for row in range(4):
        columns = list(range(1, width))
        chips += [row * width + c for c in (columns if row % 2 == 0 else columns[::-1])]
    return chips + [row * width for row in (3, 2, 1, 0)]


class Ring:
    def __init__(self, devices):
        chips = ring_order(devices)
        count = len(chips)
        ahead = [(chips[i], chips[(i + 1) % count]) for i in range(count)]
        forward = [(2 * a, 2 * b) for a, b in ahead] + [(2 * b + 1, 2 * a + 1) for a, b in ahead]
        self.forward, self.backward = forward, [(b, a) for a, b in forward]
        self.steps = count // 2

    def step(self, blocks, number):
        out = [lax.ppermute(blocks[0], "lat", self.forward)]
        if number < self.steps:
            out += [lax.ppermute(blocks[-1], "lat", self.backward)]
        return out


def complex_weight(weight, block):
    pad = ((0, LANES - block), (0, LANES - block))
    re, im = jnp.pad(weight[0], pad), jnp.pad(weight[1], pad)
    return jnp.concatenate((jnp.concatenate((re, im), 1), jnp.concatenate((-im, re), 1)), 0)


def shards(
    block_input,
    cotangent,
    first_gain,
    first_shift,
    inner_weight,
    inner_bias,
    outer_weight,
    outer_bias,
    second_gain,
    second_shift,
    up_weight,
    up_bias,
    down_weight,
    down_bias,
):
    bands, length, channels = block_input.shape
    assert bands == 1
    devices = lax.axis_size("lat")
    index = lax.axis_index("lat")
    block = inner_weight.shape[2]
    blocks = channels // block
    members = devices // blocks
    per_member = -(-(length // 2 + 1) // members)
    per_member = -(-per_member // 16) * 16
    rows = 2 * per_member
    units = up_weight.shape[0]
    tokens = -(-length // 64) * 64
    x = block_input[0]
    ring = Ring(devices)
    third = max(ring.steps - 1, 1)
    a2a = partial(lax.all_to_all, axis_name="lat", split_axis=0, concat_axis=0, tiled=True)

    fwd = np.pad(lon_table(length, members, per_member, False), ((0, 0), (0, tokens - length)))
    inv = np.pad(lon_table(length, members, per_member, True), ((0, 0), (0, tokens - length)))
    all_rows, wide = members * rows, blocks * LANES
    packed = struct((devices, rows * block // LANES, LANES), BF16)
    row_scratch = pltpu.VMEM((all_rows, wide), BF16)
    table_scratch = pltpu.VMEM((2, all_rows, tokens), BF16)
    back_scratch = pltpu.VMEM((2, tokens, all_rows), BF16)
    sems = lambda count: pltpu.SemaphoreType.DMA((count,))
    row = pltpu.VMEM((channels,), F32)
    short = pltpu.VMEM((length, channels), BF16)

    start = (index // members) * block
    def own(array):
        return lax.dynamic_slice_in_dim(array, start, block, 1)
    w1 = complex_weight(own(inner_weight), block)
    w2 = complex_weight(own(outer_weight), block)
    b1 = jnp.pad(own(inner_bias), ((0, 0), (0, LANES - block))).reshape(1, 2 * LANES)
    b2 = jnp.pad(own(outer_bias), ((0, 0), (0, LANES - block))).reshape(1, 2 * LANES)

    token = struct((tokens, channels), BF16)
    outgoing, cot = call(
        partial(first_kernel, members, block), (packed, token), [short, short, row, row, table_scratch, sems(5)],
        [HBM] * 5, x, cotangent[0], first_gain, first_shift, host_split(fwd))
    cots = [[cot], ring.step([cot], 1)]
    share = units // devices
    begin = (index // 2) * 2 * share
    up_own = lax.dynamic_slice_in_dim(up_weight, begin, 2 * share, 0)
    bias_own = lax.dynamic_slice_in_dim(up_bias, begin, 2 * share, 0)[:, None]
    down_own = lax.dynamic_slice_in_dim(down_weight, begin, 2 * share, 1).T
    incoming, cots[1], up_own, bias_own, down_own = lax.optimization_barrier(
        (a2a(outgoing), cots[1], up_own, bias_own, down_own))
    full = pltpu.VMEM((tokens, channels), BF16)
    grad_hidden = call(
        prepare_kernel, struct((tokens, units), F32),
        [full, pltpu.VMEM(down_weight.shape, BF16), sems(2)], [HBM] * 2, cot, down_weight, out_specs=PINNED)
    spectral = struct((devices * per_member, 2 * LANES), BF16)
    kept_scratch = [pltpu.VMEM(spectral.shape, BF16)] * 4 + [sems(4)]
    spectral_scratch = [pltpu.VMEM(spectral.shape, F32), pltpu.VMEM((devices, rows, LANES), F32)] + kept_scratch
    returning, *kept = call(
        partial(filter_kernel, block), (packed, spectral, spectral, spectral, spectral), spectral_scratch,
        [VMEM] * 5, incoming, w1, b1, w2, b2, out_specs=(VMEM, HBM, HBM, HBM, HBM))
    for number in range(2, third + 1):
        cots += [ring.step(cots[-1], number)]
    back, grad_hidden = lax.optimization_barrier((a2a(returning), grad_hidden))
    grad_hidden, cots[2:] = lax.optimization_barrier((grad_hidden, cots[2:]))
    residual, second, up_near = call(
        partial(second_kernel, members, block, blocks), (token, token, struct(up_weight.shape, BF16)),
        [pltpu.VMEM(packed.shape, BF16), row_scratch, back_scratch, short, row, row, row, row, sems(8)],
        [EITHER] + [HBM] * 7,
        back, x, first_gain, first_shift, second_gain, second_shift, host_split(inv.T), up_weight,
        out_specs=(VMEM, VMEM, PINNED))
    seconds = [[second], ring.step([second], 1)]

    chunk = 768
    hidden, grad_resid, grad_out = call(
        partial(mlp_kernel, members, block, chunk),
        (struct((tokens, units), BF16), struct((tokens, channels), F32), packed),
        [pltpu.VMEM((tokens, channels), F32), pltpu.VMEM((tokens, units), BF16), pltpu.VMEM((tokens, channels), F32),
         full, full, row, pltpu.VMEM((1, units), F32), table_scratch, sems(7)],
        [VMEM, PINNED, PINNED] + [HBM] * 5,
        second, up_near, grad_hidden, residual, cot, second_gain, up_bias[None], host_split(inv),
        out_specs=(HBM, HBM, VMEM), limit=20)
    block_output = (
        residual.astype(F32) + dot(hidden, down_weight, ((1,), (1,))) + down_bias
    ).astype(BF16)[None, :length]
    seconds[1], _ = lax.optimization_barrier((seconds[1], grad_out))
    for number in range(2, third):
        seconds += [ring.step(seconds[-1], number)]
    grad_in, cots[third] = lax.optimization_barrier((a2a(grad_out), cots[third]))
    cots += [ring.step(cots[-1], ring.steps)]

    grad_back, squares = call(
        partial(filter_grad_kernel, block), (packed, struct((2, 2, block, block), F32)), spectral_scratch,
        [VMEM] * 3 + [HBM] * 4, grad_in, w1, w2, *kept)
    seconds[2:], _ = lax.optimization_barrier((seconds[2:], grad_back))
    seconds += [ring.step(seconds[-1], third)]
    grad_lon = a2a(grad_back)
    seconds += [ring.step(seconds[-1], ring.steps)]
    part = block // members
    squares = squares.reshape(2, 2, members, part, block)
    member = index % members
    def piece(which):
        return lax.dynamic_index_in_dim(squares, which, 2, keepdims=False)
    total = piece(member)
    for hop in range(1, members):
        pairs = [(d, d - d % members + (d % members + hop) % members) for d in range(devices)]
        total = total + lax.ppermute(piece((member + hop) % members), "lat", pairs)

    seconds = [block for step in seconds for block in step]
    cots = [block for step in cots for block in step]
    last = len(seconds) - 3
    halves = struct((2, share, channels), F32)

    def grads(low, high, terms, after, spill=False):
        count = high - low
        stack = pltpu.VMEM((count * tokens, channels), BF16)
        sums = pltpu.VMEM((2,) + halves.shape, F32)
        return call(
            partial(grads_kernel, count, terms is not None, spill), (halves, halves),
            [stack, stack, sums, sems(2 * count + 2)],
            [HBM] * (2 * count) + [VMEM] * 3 + [EITHER] + [HBM] * len(terms or ()),
            *seconds[low:high], *cots[low:high], up_own, bias_own, down_own, after, *(terms or ()),
            out_specs=(HBM, HBM) if spill else None, limit=24)

    terms = None
    for low in range(0, last, 5):
        terms = grads(low, min(low + 5, last), terms, grad_back, True)
    grad_lon, seconds[-1], total = lax.optimization_barrier((grad_lon, seconds[-1], total))
    down_term, up_term = grads(last, last + 3, terms, grad_lon)
    core = index % 2
    swap = [(d, d ^ 1) for d in range(devices)]

    def halved(term):
        mine = lax.dynamic_index_in_dim(term, core, 0, keepdims=False)
        other = lax.dynamic_index_in_dim(term, 1 - core, 0, keepdims=False)
        return mine, lax.ppermute(other, "lat", swap)

    input_grad = call(
        partial(last_kernel, members, block, blocks), struct((length, channels), BF16),
        [row_scratch, back_scratch, short, row, pltpu.VMEM((tokens, channels), F32), sems(4)], [VMEM] + [HBM] * 4,
        grad_lon, x, first_gain, grad_resid, host_split(fwd.T))[None]
    down_mine, down_other = halved(down_term)
    down_mine, input_grad = lax.optimization_barrier((down_mine, input_grad))
    down_part = call(turn_kernel, struct((channels, share), BF16), [], [VMEM] * 2, down_mine, down_other)
    down_rows = a2a(down_part.reshape(devices, channels // devices, share))
    up_mine, up_other = halved(up_term)
    down_rows, up_other = lax.optimization_barrier((down_rows, up_other))
    down_grad = call(join_kernel, struct((channels // devices, units), F32), [], [VMEM], down_rows)
    up_grad = up_mine + up_other
    return (block_output, input_grad, up_grad, down_grad, total[0], total[1])


def solution(mesh):
    tokens = P(("rep", "lat"), None, None)
    return jax.shard_map(
        shards,
        mesh=mesh,
        in_specs=(tokens, tokens) + (P(),) * 12,
        out_specs=(
            tokens,
            tokens,
            P(("rep", "lat"), None),
            P(("rep", "lat"), None),
            P("rep", "lat", None),
            P("rep", "lat", None),
        ),
        check_vma=False,
    )
```

```python
from functools import partial
import math

import jax
import jax.numpy as jnp
import ml_dtypes
import numpy as np
from jax import lax
from jax.experimental import pallas as pl
from jax.experimental.pallas import tpu as pltpu
from jax.sharding import PartitionSpec as P

EPS = 1e-05
SHRINK = 0.01
LANES = 128
BF16 = jnp.bfloat16
F32 = jnp.float32


def dot(a, b, dims=((1,), (0,))):
    return lax.dot_general(a, b, (dims, ((), ())), preferred_element_type=F32)


def split(values):
    high = values.astype(BF16)
    return high, (values - high.astype(F32)).astype(BF16)


def dot3(a, b):
    return dot(a[0], b[0]) + (dot(a[0], b[1]) + dot(a[1], b[0]))


def host_split(table):
    high = table.astype(np.float32).astype(ml_dtypes.bfloat16)
    low = (table - high.astype(np.float64)).astype(np.float32).astype(ml_dtypes.bfloat16)
    return jnp.asarray(np.stack((high, low)))


def lon_table(length, members, per_member, weighted):
    count = length // 2 + 1
    mode = np.arange(members * per_member).reshape(members, 1, per_member, 1)
    angle = 2.0 * np.pi / length * ((mode * np.arange(length)) % length)
    weight = (mode < count) / math.sqrt(length)
    edge = (mode == 0) | (2 * mode == length)
    if weighted:
        weight = weight * np.where(edge, 1.0, 2.0)
    sine = np.where(edge, 0.0, -np.sin(angle))
    table = np.concatenate((np.cos(angle) * weight, sine * weight), axis=1)
    return table.reshape(members * 2 * per_member, length)


def moments(values):
    average = jnp.mean(values, axis=-1, keepdims=True)
    centered = values - average
    variance = jnp.mean(centered * centered, axis=-1, keepdims=True)
    scale = lax.rsqrt(variance + EPS)
    return centered * scale, scale


def norm_grad(unit, scale, grad_unit):
    mean_grad = jnp.mean(grad_unit, axis=-1, keepdims=True)
    mean_dot = jnp.mean(grad_unit * unit, axis=-1, keepdims=True)
    return scale * (grad_unit - mean_grad - unit * mean_dot)


def gelu_and_slope(values):
    magnitude = jnp.abs(values) * math.sqrt(0.5)
    t = 1.0 / (1.0 + 0.3275911 * magnitude)
    bell = jnp.exp(-0.5 * values * values)
    tail = t * (0.127414796 + t * (-0.142248368 + t * (0.7107068705 + t * (-0.7265760135 + t * 0.5307027145))))
    tail = tail * bell
    phi = jnp.where(values < 0.0, tail, 1.0 - tail)
    return values * phi, phi + values * (bell * (1.0 / math.sqrt(2.0 * math.pi)))


def fft(pairs, sign):
    n = len(pairs)
    if n == 1:
        return pairs
    assert n % 2 == 0
    even, odd = fft(pairs[0::2], sign), fft(pairs[1::2], sign)
    low, high = [], []
    for k in range(n // 2):
        (er, ei), (xr, xi) = even[k], odd[k]
        if k == 0:
            tr, ti = xr, xi
        elif 4 * k == n:
            tr, ti = (-xi, xr) if sign > 0 else (xi, -xr)
        else:
            c, s = math.cos(2.0 * math.pi * k / n), sign * math.sin(2.0 * math.pi * k / n)
            tr, ti = xr * c - xi * s, xr * s + xi * c
        low.append((er + tr, ei + ti))
        high.append((er - tr, ei - ti))
    return low + high


def spread(values, block):
    zeros = jnp.zeros((values.shape[0], LANES - block), values.dtype)
    pieces = []
    for b in range(values.shape[1] // block):
        pieces += [jnp.concatenate((values[:, b * block:(b + 1) * block], zeros), axis=1)]
    return jnp.concatenate(pieces, axis=1)


def compact(values, block, blocks):
    return jnp.concatenate([values[:, b * LANES:b * LANES + block] for b in range(blocks)], axis=1)


def lane_mask(shape, low, high):
    lane = lax.broadcasted_iota(jnp.int32, shape, 1)
    return (lane >= low) & (lane < high)


def pack(values, block):
    rows = values.shape[0]
    free = LANES - block
    kept = rows * block // LANES
    spare = rows - kept
    out = []
    for k in range(kept // spare):
        moved = pltpu.roll(values[kept:], block - k * free, 1)
        own = values[k * spare:(k + 1) * spare]
        out.append(jnp.where(lane_mask(own.shape, 0, block), own, moved))
    return jnp.concatenate(out, axis=0)


def unpack(values, block):
    kept = values.shape[0]
    free = LANES - block
    spare = kept * free // block
    last = jnp.zeros((spare, LANES), values.dtype)
    for k in range(kept // spare):
        moved = pltpu.roll(values[k * spare:(k + 1) * spare], LANES - block + k * free, 1)
        last = jnp.where(lane_mask(moved.shape, k * free, (k + 1) * free), moved, last)
    first = jnp.where(lane_mask(values.shape, 0, block), values, 0.0)
    return jnp.concatenate((first, last), axis=0)


def gather_blocks(ref, members, block, out_ref):
    devices = ref.shape[0]
    rows = out_ref.shape[0] // members
    for d in range(devices):
        b, r = d // members, d % members
        out_ref[r * rows:(r + 1) * rows, b * LANES:(b + 1) * LANES] = unpack(ref[d].astype(F32), block).astype(BF16)
    return out_ref[...]


def scatter_blocks(values, members, block, ref):
    rows = values.shape[0] // members
    for d in range(ref.shape[0]):
        b, r = d // members, d % members
        piece = values[r * rows:(r + 1) * rows, b * LANES:(b + 1) * LANES]
        ref[d] = pack(piece, block).astype(BF16)


def pad_rows(values, rows):
    return jnp.concatenate((values, jnp.zeros((rows - values.shape[0], values.shape[1]), values.dtype)), axis=0)


def fetch(pairs, sems):
    copies = [pltpu.make_async_copy(src, dst, sems.at[i]) for i, (src, dst) in enumerate(pairs)]
    for copy in copies:
        copy.start()
    return copies


def first_kernel(members, block, x_hbm, cot_hbm, gain_hbm, shift_hbm, table_hbm, out_ref, pad_ref,
                 x_ref, cot_ref, gain_ref, shift_ref, table_ref, sems):
    copies = fetch(((x_hbm, x_ref), (gain_hbm, gain_ref), (shift_hbm, shift_ref), (table_hbm, table_ref),
                    (cot_hbm, cot_ref)), sems)
    copies[0].wait()
    unit, _ = moments(x_ref[...].astype(F32))
    copies[1].wait()
    copies[2].wait()
    first = unit * gain_ref[...][None] + shift_ref[...][None]
    wide = split(spread(pad_rows(first, pad_ref.shape[0]), block))
    copies[3].wait()
    scatter_blocks(dot3((table_ref[0], table_ref[1]), wide), members, block, out_ref)
    copies[4].wait()
    pad_ref[...] = pad_rows(cot_ref[...].astype(F32), pad_ref.shape[0]).astype(BF16)


def load_transform(ref, block, sign, wide_ref, rows_ref):
    devices, rows, _ = rows_ref.shape
    half = rows // 2
    factor = 1.0 / math.sqrt(devices)
    for h in range(devices):
        rows_ref[h] = unpack(ref[h].astype(F32) * factor, block)
    for row in range(0, half, 8):
        pairs = [(rows_ref[h, row:row + 8], rows_ref[h, half + row:half + row + 8]) for h in range(devices)]
        for h, (re, im) in enumerate(fft(pairs, sign)):
            wide_ref[h * half + row:h * half + row + 8, :LANES] = re
            wide_ref[h * half + row:h * half + row + 8, LANES:] = im


def store_transform(wide_ref, block, sign, ref, rows_ref):
    devices, rows, _ = rows_ref.shape
    half = rows // 2
    factor = 1.0 / math.sqrt(devices)
    for row in range(0, half, 8):
        pairs = [
            (wide_ref[h * half + row:h * half + row + 8, :LANES], wide_ref[h * half + row:h * half + row + 8, LANES:])
            for h in range(devices)
        ]
        for h, (re, im) in enumerate(fft(pairs, sign)):
            rows_ref[h, row:row + 8] = re
            rows_ref[h, half + row:half + row + 8] = im
    for h in range(devices):
        ref[h] = (pack(rows_ref[h], block) * factor).astype(BF16)


def filter_kernel(block, in_ref, w1_ref, b1_ref, w2_ref, b2_ref,
                  out_ref, spec_hbm, hid_hbm, slope_hbm, shrink_hbm, wide_ref, rows_ref,
                  spec_ref, hid_ref, slope_ref, shrink_ref, sems):
    def keep(which, ref, hbm):
        copy = pltpu.make_async_copy(ref, hbm, sems.at[which])
        copy.start()
        return copy

    load_transform(in_ref, block, -1.0, wide_ref, rows_ref)
    spectrum = split(wide_ref[...])
    spec_ref[...] = spectrum[0]
    copies = [keep(0, spec_ref, spec_hbm)]
    pre = dot3(spectrum, split(w1_ref[...])) + b1_ref[...]
    inner, slope = gelu_and_slope(pre)
    slope_ref[...] = slope.astype(BF16)
    inner = split(inner)
    hid_ref[...] = inner[0]
    copies += [keep(1, hid_ref, hid_hbm), keep(2, slope_ref, slope_hbm)]
    outer = dot3(inner, split(w2_ref[...])) + b2_ref[...]
    bend = jnp.tanh(outer / SHRINK)
    shrink_ref[...] = (bend * bend).astype(BF16)
    copies += [keep(3, shrink_ref, shrink_hbm)]
    wide_ref[...] = outer - SHRINK * bend
    store_transform(wide_ref, block, 1.0, out_ref, rows_ref)
    for copy in copies:
        copy.wait()


def complex_grad(grad, block):
    a, b = slice(0, block), slice(LANES, LANES + block)
    return grad[a, a] + grad[b, b], grad[a, b] - grad[b, a]


def filter_grad_kernel(block, in_ref, w1_hbm, w2_hbm, spec_hbm, hid_hbm, slope_hbm, shrink_hbm, out_ref, grads_ref,
                       wide_ref, rows_ref, spec_ref, hid_ref, slope_ref, shrink_ref, w1_ref, w2_ref, sems):
    copies = fetch(((shrink_hbm, shrink_ref), (slope_hbm, slope_ref), (spec_hbm, spec_ref), (hid_hbm, hid_ref),
                    (w2_hbm, w2_ref), (w1_hbm, w1_ref)), sems)
    load_transform(in_ref, block, -1.0, wide_ref, rows_ref)
    copies[0].wait()
    copies[4].wait()
    copies[5].wait()
    grad_outer = (wide_ref[...] * shrink_ref[...].astype(F32)).astype(BF16)
    grad_inner = dot(grad_outer, w2_ref[...].astype(BF16), ((1,), (1,)))
    copies[1].wait()
    grad_pre = (grad_inner * slope_ref[...].astype(F32)).astype(BF16)
    wide_ref[...] = dot(grad_pre, w1_ref[...].astype(BF16), ((1,), (1,)))
    store_transform(wide_ref, block, 1.0, out_ref, rows_ref)
    copies[2].wait()
    re, im = complex_grad(dot(spec_ref[...], grad_pre, ((0,), (0,))), block)
    grads_ref[0, 0] = re
    grads_ref[0, 1] = im
    copies[3].wait()
    re, im = complex_grad(dot(hid_ref[...], grad_outer, ((0,), (0,))), block)
    grads_ref[1, 0] = re
    grads_ref[1, 1] = im


def second_kernel(members, block, blocks, in_hbm, x_hbm, gain1_hbm, shift1_hbm, gain2_hbm, shift2_hbm, table_hbm,
                  up_hbm, resid_ref, second_ref, up_ref, in_ref, rows_ref, table_ref, x_ref, gain1_ref, shift1_ref, gain2_ref, shift2_ref,
                  sems):
    copies = fetch(((x_hbm, x_ref), (gain1_hbm, gain1_ref), (shift1_hbm, shift1_ref), (table_hbm, table_ref),
                    (gain2_hbm, gain2_ref), (shift2_hbm, shift2_ref), (in_hbm, in_ref), (up_hbm, up_ref)), sems)
    copies[6].wait()
    back = gather_blocks(in_ref, members, block, rows_ref)
    for copy in copies[:3]:
        copy.wait()
    x = x_ref[...].astype(F32)
    unit, _ = moments(x)
    x = pad_rows(x + (unit * gain1_ref[...][None] + shift1_ref[...][None]), resid_ref.shape[0])
    for copy in copies[3:6]:
        copy.wait()
    filtered = compact(dot(table_ref[0], back) + dot(table_ref[1], back), block, blocks)
    residual = (x + filtered).astype(BF16)
    resid_ref[...] = residual
    unit, _ = moments(residual.astype(F32))
    second = unit * gain2_ref[...][None] + shift2_ref[...][None]
    second_ref[...] = pad_rows(second[:x_ref.shape[0]], resid_ref.shape[0]).astype(BF16)
    copies[7].wait()


def prepare_kernel(cot_hbm, down_hbm, ghid_ref, cot_ref, down_ref, sems):
    for copy in fetch(((cot_hbm, cot_ref), (down_hbm, down_ref)), sems):
        copy.wait()
    ghid_ref[...] = dot(cot_ref[...], down_ref[...])


def mlp_kernel(members, block, chunk, second_ref, up_ref, ghid_ref, resid_hbm, cot_hbm, gain_hbm, upb_hbm, table_hbm,
               hid_hbm, gres_hbm, out_ref, acc_ref, hid_ref, gres_ref, resid_ref, cot_ref, gain_ref, upb_ref, table_ref,
               sems):
    copies = fetch(((upb_hbm, upb_ref), (resid_hbm, resid_ref), (cot_hbm, cot_ref), (gain_hbm, gain_ref),
                    (table_hbm, table_ref)), sems)
    copies[0].wait()
    for start in range(0, up_ref.shape[0], chunk):
        part = slice(start, start + chunk)
        pre = dot(second_ref[...], up_ref[part], ((1,), (1,))) + upb_ref[:, part]
        hidden, slope = gelu_and_slope(pre)
        hid_ref[:, part] = hidden.astype(BF16)
        grad_pre = (ghid_ref[:, part] * slope).astype(BF16)
        term = dot(grad_pre, up_ref[part])
        if start == 0:
            acc_ref[...] = term
        else:
            acc_ref[...] += term
    hid_copy = pltpu.make_async_copy(hid_ref, hid_hbm, sems.at[5])
    hid_copy.start()
    for copy in copies[1:]:
        copy.wait()
    unit, scale = moments(resid_ref[...].astype(F32))
    grad = cot_ref[...].astype(F32) + norm_grad(unit, scale, acc_ref[...] * gain_ref[...][None])
    gres_ref[...] = grad
    gres_copy = pltpu.make_async_copy(gres_ref, gres_hbm, sems.at[6])
    gres_copy.start()
    wide = split(spread(grad, block))
    scatter_blocks(dot3((table_ref[0], table_ref[1]), wide), members, block, out_ref)
    hid_copy.wait()
    gres_copy.wait()


def last_kernel(members, block, blocks, in_ref, x_hbm, gain_hbm, gres_hbm, table_hbm, out_ref, rows_ref, table_ref,
                x_ref, gain_ref, gres_ref, sems):
    copies = fetch(((x_hbm, x_ref), (gain_hbm, gain_ref), (gres_hbm, gres_ref), (table_hbm, table_ref)), sems)
    back = gather_blocks(in_ref, members, block, rows_ref)
    for copy in copies:
        copy.wait()
    unit, scale = moments(x_ref[...].astype(F32))
    length = unit.shape[0]
    gres = gres_ref[:length]
    grad = compact(dot(table_ref[0], back) + dot(table_ref[1], back), block, blocks)[:length]
    out_ref[...] = (gres + norm_grad(unit, scale, (grad + gres) * gain_ref[...][None])).astype(BF16)


def token_chunks(ref, width=384):
    tokens = ref.shape[0]
    return [slice(start, min(start + width, tokens)) for start in range(0, tokens, width)]


def fetch_blocks(blocks, ref, sems, base):
    size = ref.shape[0] // len(blocks)
    copies = []
    for i, block in enumerate(blocks):
        copy = pltpu.make_async_copy(block, ref.at[i * size:(i + 1) * size], sems.at[base + i])
        copy.start()
        copies += [copy]
    return copies


def wait_blocks(copies, part, size):
    for i in range(part.start // size, part.stop // size):
        copies[i].wait()


def grads_kernel(count, has_terms, spill, *refs):
    refs = list(refs)
    take = lambda n: [refs.pop(0) for _ in range(n)]
    seconds, cots = take(count), take(count)
    up_ref, bias_ref, down_ref, _ = take(4)
    terms = take(2 * has_terms)
    outs = take(2)
    second_ref, cot_ref, sums_ref, sems = take(4)
    size = second_ref.shape[0] // count
    second_copies = fetch_blocks(seconds, second_ref, sems, 0)
    cot_copies = fetch_blocks(cots, cot_ref, sems, count)
    term_copies = [
        pltpu.make_async_copy(term, sums_ref.at[i], sems.at[2 * count + i]) for i, term in enumerate(terms)]
    for copy in term_copies:
        copy.start()
    sums = [0.0, 0.0]
    for part in token_chunks(second_ref):
        wait_blocks(second_copies, part, size)
        hidden, slope = gelu_and_slope(dot(up_ref[...], second_ref[part], ((1,), (1,))) + bias_ref[...])
        wait_blocks(cot_copies, part, size)
        sums[0] = sums[0] + dot(hidden.astype(BF16), cot_ref[part])
        grad_hidden = dot(down_ref[...], cot_ref[part], ((1,), (1,)))
        sums[1] = sums[1] + dot((grad_hidden * slope).astype(BF16), second_ref[part])
    for copy in term_copies:
        copy.wait()
    half = sums[0].shape[0] // 2
    out_copies = []
    for i, (out, total) in enumerate(zip(outs, sums)):
        if has_terms:
            total = total + jnp.concatenate((sums_ref[i, 0], sums_ref[i, 1]), axis=0)
        target = sums_ref.at[i] if spill else out
        target[0] = total[:half]
        target[1] = total[half:]
        if spill:
            out_copies += [pltpu.make_async_copy(sums_ref.at[i], out, sems.at[2 * count + i])]
            out_copies[-1].start()
    for copy in out_copies:
        copy.wait()


def join_kernel(in_ref, out_ref):
    width = in_ref.shape[2]
    for d in range(in_ref.shape[0]):
        out_ref[:, d * width:(d + 1) * width] = in_ref[d].astype(F32)


def turn_kernel(own_ref, other_ref, out_ref):
    out_ref[...] = (own_ref[...] + other_ref[...]).T.astype(BF16)


def struct(shape, dtype):
    return jax.ShapeDtypeStruct(shape, dtype)


VMEM = pl.BlockSpec(memory_space=pltpu.VMEM)
PINNED = pl.BlockSpec(memory_space=pltpu.VMEM)
HBM = pl.BlockSpec(memory_space=pltpu.HBM)
EITHER = pl.BlockSpec(memory_space=pl.ANY)


def call(kernel, out, scratch, in_specs, *args, out_specs=None, limit=12, cost=1):
    if out_specs is None:
        out_specs = jax.tree.map(lambda _: VMEM, out)
    flat = out_specs if isinstance(out_specs, tuple) else (out_specs,)
    shapes = out if isinstance(out, tuple) else (out,)
    shapes = tuple(
        pltpu.HBM(o.shape, o.dtype) if spec is HBM else pltpu.VMEM(o.shape, o.dtype) if spec is PINNED else o
        for o, spec in zip(shapes, flat))
    out = shapes if isinstance(out, tuple) else shapes[0]
    spaces = {id(HBM): pltpu.HBM, id(PINNED): pltpu.VMEM}
    args = [
        pltpu.with_memory_space_constraint(a, spaces[id(spec)]) if id(spec) in spaces else a
        for a, spec in zip(args, in_specs)]
    return pl.pallas_call(
        kernel, out_shape=out, scratch_shapes=scratch, in_specs=in_specs, out_specs=out_specs,
        cost_estimate=pl.CostEstimate(flops=cost, transcendentals=0, bytes_accessed=cost),
        compiler_params=pltpu.CompilerParams(vmem_limit_bytes=limit << 20))(*args)


def ring_order(devices):
    width = devices // 8
    chips = []
    for row in range(4):
        columns = list(range(1, width))
        chips += [row * width + c for c in (columns if row % 2 == 0 else columns[::-1])]
    return chips + [row * width for row in (3, 2, 1, 0)]


class Ring:
    def __init__(self, devices):
        chips = ring_order(devices)
        count = len(chips)
        ahead = [(chips[i], chips[(i + 1) % count]) for i in range(count)]
        forward = [(2 * a, 2 * b) for a, b in ahead] + [(2 * b + 1, 2 * a + 1) for a, b in ahead]
        self.forward, self.backward = forward, [(b, a) for a, b in forward]
        self.steps = count // 2

    def step(self, blocks, number):
        out = [lax.ppermute(blocks[0], "lat", self.forward)]
        if number < self.steps:
            out += [lax.ppermute(blocks[-1], "lat", self.backward)]
        return out


def complex_weight(weight, block):
    pad = ((0, LANES - block), (0, LANES - block))
    re, im = jnp.pad(weight[0], pad), jnp.pad(weight[1], pad)
    return jnp.concatenate((jnp.concatenate((re, im), 1), jnp.concatenate((-im, re), 1)), 0)


def shards(
    block_input,
    cotangent,
    first_gain,
    first_shift,
    inner_weight,
    inner_bias,
    outer_weight,
    outer_bias,
    second_gain,
    second_shift,
    up_weight,
    up_bias,
    down_weight,
    down_bias,
):
    bands, length, channels = block_input.shape
    assert bands == 1
    devices = lax.axis_size("lat")
    index = lax.axis_index("lat")
    block = inner_weight.shape[2]
    blocks = channels // block
    members = devices // blocks
    per_member = -(-(length // 2 + 1) // members)
    per_member = -(-per_member // 16) * 16
    rows = 2 * per_member
    units = up_weight.shape[0]
    tokens = -(-length // 64) * 64
    x = block_input[0]
    ring = Ring(devices)
    third = max(ring.steps - 1, 1)
    a2a = partial(lax.all_to_all, axis_name="lat", split_axis=0, concat_axis=0, tiled=True)

    fwd = np.pad(lon_table(length, members, per_member, False), ((0, 0), (0, tokens - length)))
    inv = np.pad(lon_table(length, members, per_member, True), ((0, 0), (0, tokens - length)))
    all_rows, wide = members * rows, blocks * LANES
    packed = struct((devices, rows * block // LANES, LANES), BF16)
    row_scratch = pltpu.VMEM((all_rows, wide), BF16)
    table_scratch = pltpu.VMEM((2, all_rows, tokens), BF16)
    back_scratch = pltpu.VMEM((2, tokens, all_rows), BF16)
    sems = lambda count: pltpu.SemaphoreType.DMA((count,))
    row = pltpu.VMEM((channels,), F32)
    short = pltpu.VMEM((length, channels), BF16)

    start = (index // members) * block
    def own(array):
        return lax.dynamic_slice_in_dim(array, start, block, 1)
    w1 = complex_weight(own(inner_weight), block)
    w2 = complex_weight(own(outer_weight), block)
    b1 = jnp.pad(own(inner_bias), ((0, 0), (0, LANES - block))).reshape(1, 2 * LANES)
    b2 = jnp.pad(own(outer_bias), ((0, 0), (0, LANES - block))).reshape(1, 2 * LANES)

    token = struct((tokens, channels), BF16)
    outgoing, cot = call(
        partial(first_kernel, members, block), (packed, token), [short, short, row, row, table_scratch, sems(5)],
        [HBM] * 5, x, cotangent[0], first_gain, first_shift, host_split(fwd))
    cots = [[cot], ring.step([cot], 1)]
    share = units // devices
    begin = (index // 2) * 2 * share
    up_own = lax.dynamic_slice_in_dim(up_weight, begin, 2 * share, 0)
    bias_own = lax.dynamic_slice_in_dim(up_bias, begin, 2 * share, 0)[:, None]
    down_own = lax.dynamic_slice_in_dim(down_weight, begin, 2 * share, 1).T
    incoming, cots[1], up_own, bias_own, down_own = lax.optimization_barrier(
        (a2a(outgoing), cots[1], up_own, bias_own, down_own))
    full = pltpu.VMEM((tokens, channels), BF16)
    grad_hidden = call(
        prepare_kernel, struct((tokens, units), F32),
        [full, pltpu.VMEM(down_weight.shape, BF16), sems(2)], [HBM] * 2, cot, down_weight, out_specs=PINNED)
    spectral = struct((devices * per_member, 2 * LANES), BF16)
    kept_scratch = [pltpu.VMEM(spectral.shape, BF16)] * 4 + [sems(4)]
    spectral_scratch = [pltpu.VMEM(spectral.shape, F32), pltpu.VMEM((devices, rows, LANES), F32)] + kept_scratch
    returning, *kept = call(
        partial(filter_kernel, block), (packed, spectral, spectral, spectral, spectral), spectral_scratch,
        [VMEM] * 5, incoming, w1, b1, w2, b2, out_specs=(VMEM, HBM, HBM, HBM, HBM))
    for number in range(2, third + 1):
        cots += [ring.step(cots[-1], number)]
    back, grad_hidden = lax.optimization_barrier((a2a(returning), grad_hidden))
    grad_hidden, cots[2:] = lax.optimization_barrier((grad_hidden, cots[2:]))
    residual, second, up_near = call(
        partial(second_kernel, members, block, blocks), (token, token, struct(up_weight.shape, BF16)),
        [pltpu.VMEM(packed.shape, BF16), row_scratch, back_scratch, short, row, row, row, row, sems(8)],
        [EITHER] + [HBM] * 7,
        back, x, first_gain, first_shift, second_gain, second_shift, host_split(inv.T), up_weight,
        out_specs=(VMEM, VMEM, PINNED))
    seconds = [[second], ring.step([second], 1)]

    chunk = 768
    hidden, grad_resid, grad_out = call(
        partial(mlp_kernel, members, block, chunk),
        (struct((tokens, units), BF16), struct((tokens, channels), F32), packed),
        [pltpu.VMEM((tokens, channels), F32), pltpu.VMEM((tokens, units), BF16), pltpu.VMEM((tokens, channels), F32),
         full, full, row, pltpu.VMEM((1, units), F32), table_scratch, sems(7)],
        [VMEM, PINNED, PINNED] + [HBM] * 5,
        second, up_near, grad_hidden, residual, cot, second_gain, up_bias[None], host_split(inv),
        out_specs=(HBM, HBM, VMEM), limit=20)
    block_output = (
        residual.astype(F32) + dot(hidden, down_weight, ((1,), (1,))) + down_bias
    ).astype(BF16)[None, :length]
    seconds[1], _ = lax.optimization_barrier((seconds[1], grad_out))
    for number in range(2, third):
        seconds += [ring.step(seconds[-1], number)]
    cots += [ring.step(cots[-1], ring.steps)]
    grad_out, cots[-1] = lax.optimization_barrier((grad_out, cots[-1]))
    grad_in = a2a(grad_out)

    grad_back, squares = call(
        partial(filter_grad_kernel, block), (packed, struct((2, 2, block, block), F32)), spectral_scratch[:-1] + [pltpu.VMEM(w1.shape, F32)] * 2 + [sems(6)],
        [VMEM] + [HBM] * 6, grad_in, w1, w2, *kept)
    seconds[2:], _ = lax.optimization_barrier((seconds[2:], grad_back))
    seconds += [ring.step(seconds[-1], third)]
    grad_lon = a2a(grad_back)
    seconds += [ring.step(seconds[-1], ring.steps)]
    part = block // members
    squares = squares.reshape(2, 2, members, part, block)
    member = index % members
    def piece(which):
        return lax.dynamic_index_in_dim(squares, which, 2, keepdims=False)
    total = piece(member)
    for hop in range(1, members):
        pairs = [(d, d - d % members + (d % members + hop) % members) for d in range(devices)]
        total = total + lax.ppermute(piece((member + hop) % members), "lat", pairs)

    seconds = [block for step in seconds for block in step]
    cots = [block for step in cots for block in step]
    last = len(seconds) - 3
    halves = struct((2, share, channels), F32)

    def grads(low, high, terms, after, spill=False):
        count = high - low
        stack = pltpu.VMEM((count * tokens, channels), BF16)
        sums = pltpu.VMEM((2,) + halves.shape, F32)
        return call(
            partial(grads_kernel, count, terms is not None, spill), (halves, halves),
            [stack, stack, sums, sems(2 * count + 2)],
            [HBM] * (2 * count) + [VMEM] * 3 + [EITHER] + [HBM] * len(terms or ()),
            *seconds[low:high], *cots[low:high], up_own, bias_own, down_own, after, *(terms or ()),
            out_specs=(HBM, HBM) if spill else None, limit=24)

    terms = None
    for low in range(0, last, 5):
        terms = grads(low, min(low + 5, last), terms, grad_back, True)
    grad_lon, seconds[-1], total = lax.optimization_barrier((grad_lon, seconds[-1], total))
    down_term, up_term = grads(last, last + 3, terms, grad_lon)
    core = index % 2
    swap = [(d, d ^ 1) for d in range(devices)]

    def halved(term):
        mine = lax.dynamic_index_in_dim(term, core, 0, keepdims=False)
        other = lax.dynamic_index_in_dim(term, 1 - core, 0, keepdims=False)
        return mine, lax.ppermute(other, "lat", swap)

    input_grad = call(
        partial(last_kernel, members, block, blocks), struct((length, channels), BF16),
        [row_scratch, back_scratch, short, row, pltpu.VMEM((tokens, channels), F32), sems(4)], [VMEM] + [HBM] * 4,
        grad_lon, x, first_gain, grad_resid, host_split(fwd.T))[None]
    down_mine, down_other = halved(down_term)
    down_mine, input_grad = lax.optimization_barrier((down_mine, input_grad))
    down_part = call(turn_kernel, struct((channels, share), BF16), [], [VMEM] * 2, down_mine, down_other)
    down_rows = a2a(down_part.reshape(devices, channels // devices, share))
    up_mine, up_other = halved(up_term)
    down_rows, up_other = lax.optimization_barrier((down_rows, up_other))
    down_grad = call(join_kernel, struct((channels // devices, units), F32), [], [VMEM], down_rows)
    up_grad = up_mine + up_other
    return (block_output, input_grad, up_grad, down_grad, total[0], total[1])


def solution(mesh):
    tokens = P(("rep", "lat"), None, None)
    return jax.shard_map(
        shards,
        mesh=mesh,
        in_specs=(tokens, tokens) + (P(),) * 12,
        out_specs=(
            tokens,
            tokens,
            P(("rep", "lat"), None),
            P(("rep", "lat"), None),
            P("rep", "lat", None),
            P("rep", "lat", None),
        ),
        check_vma=False,
    )
```
